512 devices in a mesh: seq: 64 (over y, z), trk: 8 (over x, core).
Axes of the slice: x: 4, y: 8, z: 8, core: 2. Of those that a mesh axis runs over, the one named last changes fastest.
Arguments:
- embeddings: bfloat16 [4, 8192, 1920], P(None, 'seq', 'trk'), may hold values from -16 to 16
- head: bfloat16 [1920, 4096], P(None, 'trk'), may hold values from -0.125 to 0.125
- exon_starts: int32 [4, 128, 8], replicated, may hold values from 0 to 8184, as said below
- exon_lengths: int32 [4, 128, 8], replicated, may hold values from 1 to 8, as said below
- gene_owner: int32 [4, 128], replicated, may hold values from 0 to 63, as said below
- gene_targets: float32 [4, 256, 4096], P(None, 'seq', 'trk'), may hold values from 2 to 400, as said below
Outputs:
- gene_pred: float32 [4, 256, 4096], P(None, 'seq', 'trk')
- loss: float32 [4, 4096], P(None, 'trk')
- grad_head: float32 [1920, 4096], P('seq', 'trk')
The draws below stay inside these ranges and needn't reach their ends.
Inputs may be any that keep to these rules, and one draw needn't show every extreme that they name: `exon_starts`: each gene has 8 exon blocks; blocks may intersect. Some block of each window starts at 0 and some at 8184. `exon_lengths`: some block of each window has length 8. `gene_owner`: in each window no owner holds more than 4 genes, and some owner holds exactly 4. `gene_targets`: entries of empty slots are read by nothing.
All inputs are finite; a program needn't handle non-finite values.
Results may differ from the reference program's by a relative error of at most 0.0041.
Values may be sent and summed in bfloat16 or wider, within the bound.
No kernel may reach another device: no remote copies, remote signals or barrier semaphores. Data moves between devices by JAX's collectives and lax.ppermute only.
A program may use at most 64 MiB of HBM per device.

```python
import jax
import jax.numpy as jnp
from jax import lax

D = 1920
TRACKS = 4096
WINDOWS = 4
CAP = 4
EXONS = 8
EXON_MAX = 8
BINS = 8192
GENES = 128
SLOTS = 256


def draw_exon_starts(key, part):
    first_key, second_key = jax.random.split(jax.random.fold_in(key, 11))
    reach = BINS // 4
    upper = BINS - EXON_MAX
    anchor = jax.random.randint(first_key, (WINDOWS, GENES, 1), 0, upper - reach + 1)
    offset = jax.random.randint(second_key, (WINDOWS, GENES, EXONS), 0, reach + 1)
    starts = anchor + offset
    starts = starts.at[:, 0, 0].set(0)
    starts = starts.at[:, 0, 1].set(upper)
    return starts.astype(jnp.int32)


def draw_exon_lengths(key, part):
    lengths = jax.random.randint(jax.random.fold_in(key, 23), (WINDOWS, GENES, EXONS), 1, EXON_MAX + 1)
    lengths = lengths.at[:, 0, 0].set(EXON_MAX)
    return lengths.astype(jnp.int32)


def draw_gene_owner(key, part):
    window_keys = jax.random.split(jax.random.fold_in(key, 37), WINDOWS)
    owners_total = SLOTS // CAP

    def single(window_key):
        pick_key, perm_key, order_key = jax.random.split(window_key, 3)
        busiest = jax.random.randint(pick_key, (), 0, owners_total)
        slot_owner = jax.random.permutation(perm_key, SLOTS) // CAP
        ordering = jnp.argsort((slot_owner == busiest).astype(jnp.int32), stable=True)
        others = slot_owner[ordering][:GENES - CAP].astype(jnp.int32)
        filled = jnp.concatenate([jnp.zeros((CAP,), jnp.int32) + busiest.astype(jnp.int32), others])
        return filled[jax.random.permutation(order_key, GENES)]
    return jax.vmap(single)(window_keys).astype(jnp.int32)


def draw_gene_targets(key, part):
    second_key = jax.random.fold_in(jax.random.fold_in(key, 41), 1)
    shape = (WINDOWS, SLOTS, TRACKS)
    position = jnp.arange(SLOTS, dtype=jnp.float32) / (SLOTS - 1)
    rising = 1.0 + 2.0 * position
    base = jnp.exp(jax.random.uniform(second_key, shape, jnp.float32, jnp.log(2.0), jnp.log(40.0)))
    values = base * rising[None, :, None]
    return values.astype(jnp.float32)


def with_spikes(array, rng, source, target, shards_of, factor):
    def block_of(dim):
        return (jnp.arange(array.shape[dim]) // (array.shape[dim] // shards_of)).reshape((-1,) + (1,) * (array.ndim - 1 - dim))

    near = jax.random.permutation(rng, shards_of)[block_of(target)]
    far = (block_of(target) + shards_of // 2) % shards_of
    return jnp.where((block_of(source) == near) | (block_of(source) == far), factor * array, array)


def levels(key, extent, pieces, smallest, top_value):
    loudness, own = 1.0, jax.random.fold_in(key, 6)
    for dim, parts in pieces:
        draws = jnp.exp(jax.random.uniform(jax.random.fold_in(own, dim), (parts,), jnp.float32, smallest / len(pieces), top_value / len(pieces)))
        loudness = loudness * jnp.repeat(draws, extent[dim] // parts).reshape([-1 if axis == dim else 1 for axis in range(len(extent))])
    return loudness


def noise(rng, dims, scale, most, cuts=(), held_as=jnp.bfloat16):
    result = jax.random.normal(rng, dims, jnp.float32) * scale
    if len(cuts) > 0:
        result = levels(rng, dims, cuts, -0.22, 0.18) * result
    return jnp.clip(result, min=-most, max=most).astype(held_as)


def bell_draw_with(stream_key, shape, scale, bound, shards, heavy, kind=jnp.bfloat16):
    values = scale * jax.random.normal(stream_key, shape, jnp.float32)
    if shards:
        values = values * levels(stream_key, shape, shards, -0.22, 0.18)
    return jnp.clip(with_spikes(values, jax.random.fold_in(stream_key, 3), *heavy), -bound, bound).astype(kind)


def setup_inputs(seed: int = 0) -> dict:
    seeds = jax.random.split(jax.random.key(seed), 7)
    return {
        "embeddings": bell_draw_with(seeds[0], (WINDOWS, BINS, D), 1.0, 16.0, ((1, 64), (2, 8)), (1, 2, 64, 4.0)),
        "head": noise(seeds[1], (D, TRACKS), D ** -0.5, 0.125, ((1, 8),)),
        "exon_starts": draw_exon_starts(jax.random.fold_in(seeds[6], 71), 0),
        "exon_lengths": draw_exon_lengths(jax.random.fold_in(seeds[6], 71), 0),
        "gene_owner": draw_gene_owner(jax.random.fold_in(seeds[6], 71), 0),
        "gene_targets": draw_gene_targets(jax.random.fold_in(seeds[6], 71), 0),
    }


def slot_table(gene_owner, capacity):
    genes = gene_owner.shape[1]
    same = gene_owner[:, :, None] == gene_owner[:, None, :]
    earlier = jnp.arange(genes)[None, :] < jnp.arange(genes)[:, None]
    ahead = jnp.sum((same & earlier[None]).astype(jnp.int32), axis=2)
    return (gene_owner * capacity + ahead).astype(jnp.int32)


def coverage(starts, lengths, positions):
    where_bin = positions[None, None, None, :]
    inside = (where_bin >= starts[..., None]) & (where_bin < (starts + lengths)[..., None])
    return jnp.sum(inside.astype(jnp.float32), axis=2)


def reference(embeddings, head, exon_starts, exon_lengths, gene_owner, gene_targets):
    slot_of = slot_table(gene_owner, CAP)
    onehot = (slot_of[..., None] == jnp.arange(SLOTS, dtype=jnp.int32)).astype(jnp.float32)
    valid = jnp.sum(onehot, axis=1)
    cover = coverage(exon_starts, exon_lengths, jnp.arange(BINS, dtype=jnp.int32))
    member = jnp.einsum("wgs,wgb->wsb", onehot, cover, precision=lax.Precision.HIGHEST).astype(jnp.bfloat16)

    def forward(pair):
        rows, members = pair
        pred = jax.nn.softplus(jnp.dot(rows, head, preferred_element_type=jnp.float32)).astype(jnp.bfloat16)
        return jnp.dot(members, pred, preferred_element_type=jnp.float32)

    gene_pred = lax.map(forward, (embeddings, member))
    targets = gene_targets * valid[..., None]
    total = jnp.sum(gene_pred, axis=1)
    target_sum = jnp.sum(targets, axis=1)
    safe = jnp.where(valid[..., None] > 0, gene_pred, 1.0)
    fit = jnp.sum(targets * jnp.log(safe), axis=1)
    log_total = jnp.log(total)
    loss = (-fit + target_sum * log_total + 0.2 * (total - target_sum * log_total)) / target_sum
    scale_rows = (GENES / target_sum)[:, None, :]
    gene_grad = (scale_rows * (valid[..., None] * (0.2 + 0.8 * target_sum / total)[:, None, :] - targets / safe)).astype(jnp.bfloat16)

    def backward(carry, triple):
        rows, members, grads = triple
        logits = jnp.dot(rows, head, preferred_element_type=jnp.float32)
        spread = jnp.dot(members.T, grads, preferred_element_type=jnp.float32)
        logit_grad = (spread * jax.nn.sigmoid(logits)).astype(jnp.bfloat16)
        return carry + jnp.dot(rows.T, logit_grad, preferred_element_type=jnp.float32), None

    grad_head, _ = lax.scan(backward, jnp.zeros((D, TRACKS), jnp.float32), (embeddings, member, gene_grad))
    return gene_pred, loss, grad_head
```

```python
import jax
import jax.numpy as jnp
from jax import lax
from jax.sharding import Mesh, PartitionSpec as P

SEQ = ("y", "z")
F32 = jnp.float32
BF16 = jnp.bfloat16
MIDDLE = 28.28


def exchange(blocks, axes):
    return lax.all_to_all(blocks, axes, split_axis=0, concat_axis=0, tiled=True)


def gather(block, axes):
    size = lax.axis_size(axes)
    return exchange(jnp.broadcast_to(block[None], (size,) + block.shape), axes)


def halves(values):
    high = lax.reduce_precision(values, 8, 7)
    return high.astype(BF16), (values - high).astype(BF16)


def spread(counts):
    scaled = counts * (1.0 / MIDDLE)
    for _ in range(4):
        scaled = scaled * scaled
    return scaled


def unspread(coded):
    for _ in range(4):
        coded = jnp.sqrt(coded)
    return coded * MIDDLE


def squared(ratio):
    small = ratio < 2.0**63
    scaled = jnp.where(small, ratio, ratio * 2.0**-96)
    return jnp.where(small, scaled * scaled, -(scaled * scaled))


def rooted(coded):
    root = jnp.sqrt(jnp.abs(coded))
    return jnp.where(coded < 0, root * 2.0**96, root)


def slot_table(gene_owner, capacity):
    genes = gene_owner.shape[1]
    same = gene_owner[:, :, None] == gene_owner[:, None, :]
    earlier = jnp.arange(genes)[None, :] < jnp.arange(genes)[:, None]
    ahead = jnp.sum((same & earlier[None]).astype(jnp.int32), axis=2)
    return gene_owner * capacity + ahead


def by_place(table, places):
    windows, genes = table.shape[:2]
    held = genes // places
    split = table.reshape((windows, places, held) + table.shape[2:])
    return jnp.moveaxis(split, 1, 0).reshape((genes * windows,) + table.shape[2:])


def per_device(embeddings, head, exon_starts, exon_lengths, gene_owner, gene_targets):
    places = lax.axis_size(SEQ)
    place = lax.axis_index(SEQ)
    windows, bin_dev, channels_dev = embeddings.shape
    channels, tracks = head.shape
    genes = gene_owner.shape[1]
    capacity = gene_targets.shape[1]
    held = genes // places
    per_place = windows * held
    rows = places * per_place
    xs, cores = lax.axis_size("x"), lax.axis_size("c")

    ours = gather(embeddings.transpose(0, 2, 1), "x")
    whole = gather(ours, "c")

    row = jnp.arange(rows, dtype=jnp.int32)
    row_window = (row // held) % windows
    starts = by_place(exon_starts, places)
    ends = starts + by_place(exon_lengths, places)
    bins = place * bin_dev + jnp.arange(bin_dev, dtype=jnp.int32)
    inside = (bins >= starts[..., None]) & (bins < ends[..., None])
    cover = jnp.sum(inside.astype(F32), axis=1)
    in_window = row_window[:, None] == jnp.arange(windows)
    cover = (cover[:, None, :] * in_window[..., None].astype(F32)).astype(BF16)
    cover = cover.reshape(rows, windows * bin_dev)
    slot_of = slot_table(gene_owner, capacity)
    slot_row = by_place(slot_of, places)
    here = place * capacity + jnp.arange(capacity, dtype=jnp.int32)
    chosen = in_window[..., None] & (slot_row[:, None, None] == here)
    chosen = chosen.reshape(rows, windows * capacity)
    valid_here = jnp.any(chosen, axis=0).astype(F32)[:, None]
    targets_here = gene_targets.reshape(windows * capacity, tracks)
    targets_here = jnp.where(valid_here > 0, targets_here, 1.0)
    coded = spread(targets_here).astype(BF16)
    target_rows = jnp.dot(chosen.astype(BF16), coded, preferred_element_type=F32)
    target_part = jnp.sum((targets_here * valid_here).reshape(windows, capacity, tracks), axis=1)

    logits = jnp.einsum(
        "cxwkb,xckt->wbt",
        whole,
        head.reshape(xs, cores, channels_dev, tracks),
        preferred_element_type=F32,
    ).reshape(windows * bin_dev, tracks)
    pred = jax.nn.softplus(logits).astype(BF16)
    slope = jax.nn.sigmoid(logits)
    partial = jnp.dot(cover, pred, preferred_element_type=F32)
    total_part = jnp.sum(partial.reshape(places, windows, held, tracks), axis=(0, 2))

    piece = windows * tracks // places
    pieces = jnp.concatenate(
        [*halves(total_part.reshape(places, piece)), *halves(target_part.reshape(places, piece))], axis=1
    )
    extra = jnp.pad(pieces[:, None, :], ((0, 0), (0, per_place - 1), (0, 0)))
    sent = jnp.concatenate(
        [
            partial.astype(BF16).reshape(places, per_place, tracks),
            target_rows.astype(BF16).reshape(places, per_place, tracks),
            extra,
        ],
        axis=2,
    )
    got = jnp.sum(exchange(sent, SEQ).astype(F32), axis=0)
    gene_pred = got[:, :tracks]
    gene_tgt = unspread(got[:, tracks : 2 * tracks])
    ratio = squared(gene_tgt / gene_pred).astype(BF16)
    fit_part = jnp.sum((gene_tgt * jnp.log(gene_pred)).reshape(windows, held, tracks), axis=1)
    sums = got[0, 2 * tracks :].reshape(2, 2, piece).sum(axis=1)
    common = jnp.concatenate(halves(sums), axis=1).reshape(4 * piece)
    fit_pieces = jnp.concatenate(halves(fit_part.reshape(places, piece)), axis=1)
    extra = jnp.concatenate(
        [
            jnp.broadcast_to(common, (places, 1, 4 * piece)),
            jnp.pad(fit_pieces, ((0, 0), (0, 2 * piece)))[:, None, :],
            jnp.zeros((places, per_place - 2, 4 * piece), BF16),
        ],
        axis=1,
    )
    sent = jnp.concatenate(
        [jnp.broadcast_to(ratio, (places, per_place, tracks)), extra], axis=2
    )
    got = exchange(sent, SEQ)
    ratios = got[:, :, :tracks].reshape(rows, tracks)
    sums = got[:, 0, tracks:].astype(F32).reshape(places, 2, 2, piece).sum(axis=2)
    total = sums[:, 0].reshape(windows, tracks)
    target_sum = sums[:, 1].reshape(windows, tracks)
    fit_piece = jnp.sum(got[:, 1, tracks : tracks + 2 * piece].astype(F32), axis=0).reshape(2, piece).sum(axis=0)

    scale = genes / target_sum
    level = scale * (0.2 + 0.8 * target_sum / total)
    gene_grad = (
        level[None, :, None, :] - scale[None, :, None, :] * rooted(ratios.astype(F32)).reshape(places, windows, held, tracks)
    ).astype(BF16).reshape(rows, tracks)
    bin_grad = lax.dot_general(cover, gene_grad, (((0,), (0,)), ((), ())), preferred_element_type=F32)
    logit_grad = (bin_grad * slope).astype(BF16).reshape(windows, bin_dev, tracks)
    grad = jnp.einsum("cxwkb,wbt->xckt", whole, logit_grad, preferred_element_type=F32)
    block = channels // places
    grad = grad.astype(BF16).reshape(places, block, tracks)
    spare = jnp.concatenate(halves(fit_piece))
    spare = jnp.pad(spare, (0, tracks - 2 * piece))
    sent = jnp.concatenate(
        [grad, jnp.broadcast_to(spare, (places, 1, tracks)), jnp.zeros((places, 1, tracks), BF16)], axis=1
    )
    got = exchange(sent, SEQ)
    grad_head = jnp.sum(got[:, :block].astype(F32), axis=0)
    fit = got[:, block, : 2 * piece].astype(F32).reshape(places, 2, piece).sum(axis=1).reshape(windows, tracks)
    log_total = jnp.log(total)
    loss = (-fit + target_sum * log_total + 0.2 * (total - target_sum * log_total)) / target_sum
    back = lax.dot_general(chosen.astype(BF16), ratios, (((0,), (0,)), ((), ())), preferred_element_type=F32)
    gene_here = jnp.where(valid_here > 0, targets_here / rooted(jnp.where(valid_here > 0, back, 1.0)), 0.0)
    return (gene_here.reshape(gene_targets.shape), loss, grad_head)


def solution(mesh):
    fine = Mesh(mesh.devices.reshape(8, 8, 4, 2), ("y", "z", "x", "c"))
    return jax.shard_map(
        per_device,
        mesh=fine,
        in_specs=(P(None, SEQ, ("x", "c")), P(None, ("x", "c")), P(), P(), P(), P(None, SEQ, ("x", "c"))),
        out_specs=(P(None, SEQ, ("x", "c")), P(None, ("x", "c")), P(SEQ, ("x", "c"))),
        check_vma=False,
    )
```

```python
import jax
import jax.numpy as jnp
import numpy as np
from jax import lax
from jax.experimental import pallas as pl
from jax.experimental.pallas import tpu as pltpu
from jax.sharding import Mesh, PartitionSpec as P

SEQ = ("y", "z")
EVERY = ("y", "z", "x", "c")
F32 = jnp.float32
BF16 = jnp.bfloat16
MIDDLE = 28.28
LANES = 128
VMEM = pl.BlockSpec(memory_space=pltpu.VMEM)
SMEM = pl.BlockSpec(memory_space=pltpu.SMEM)


def exchange(blocks, axes, groups=None):
    return lax.all_to_all(blocks, axes, split_axis=0, concat_axis=0, axis_index_groups=groups, tiled=True)


def gather(block, axes):
    size = lax.axis_size(axes)
    return exchange(jnp.broadcast_to(block[None], (size,) + block.shape), axes)


def mixed_groups(shape):
    ids = np.arange(int(np.prod(shape))).reshape(shape)
    ahead, after = [], []
    for x in range(shape[2]):
        for k in range(shape[0]):
            ahead += [ids[:, k, x, 0].tolist(), ids[k, :, x, 1].tolist()]
            after += [ids[k, :, x, 0].tolist(), ids[:, k, x, 1].tolist()]
    return ahead, after


def spread(counts):
    scaled = counts * (1.0 / MIDDLE)
    for _ in range(4):
        scaled = scaled * scaled
    return scaled


def unspread(coded):
    for _ in range(4):
        coded = jnp.sqrt(coded)
    return coded * MIDDLE


def squared(ratio):
    small = ratio < 2.0**63
    scaled = jnp.where(small, ratio, ratio * 2.0**-96)
    return jnp.where(small, scaled * scaled, -(scaled * scaled))


def rooted(coded):
    root = jnp.sqrt(jnp.abs(coded))
    return jnp.where(coded < 0, root * 2.0**96, root)


def split(values):
    high = values.astype(BF16).astype(F32)
    return high, values - high


def even_rows(shape):
    return lax.broadcasted_iota(jnp.int32, shape, 0) % 2 == 0


def up(values):
    return pltpu.roll(values, values.shape[0] - 1, 0)


def down(values):
    return pltpu.roll(values, 1, 0)


def slot_table(gene_owner, capacity):
    genes = gene_owner.shape[1]
    same = gene_owner[:, :, None] == gene_owner[:, None, :]
    earlier = jnp.arange(genes)[None, :] < jnp.arange(genes)[:, None]
    ahead = jnp.sum((same & earlier[None]).astype(jnp.int32), axis=2)
    return gene_owner * capacity + ahead


def by_place(table, places):
    windows, genes = table.shape[:2]
    held = genes // places
    parts = table.reshape((windows, places, held) + table.shape[2:])
    return jnp.moveaxis(parts, 1, 0).reshape((genes * windows,) + table.shape[2:])


def cover_kernel(windows, held, at_ref, starts_ref, lengths_ref, cover_ref, turned_ref):
    exons, rows = starts_ref.shape
    bins = cover_ref.shape[1] // windows
    position = lax.broadcasted_iota(jnp.int32, (bins, rows), 0) + at_ref[0] * bins
    base = jnp.zeros((bins, rows), F32)
    for e in range(exons):
        past = position - starts_ref[e : e + 1, :]
        base += jnp.where((past >= 0) & (past < lengths_ref[e : e + 1, :]), 1.0, 0.0)
    owner = (lax.broadcasted_iota(jnp.int32, (bins, rows), 1) // held) % windows
    for w in range(windows):
        mine = jnp.where(owner == w, base, 0.0)
        turned_ref[w * bins : (w + 1) * bins, :] = mine.astype(BF16)
        cover_ref[:, w * bins : (w + 1) * bins] = mine.T.astype(BF16)


def forward_kernel(whole_ref, head_ref, cover_ref, target_ref, tsum_ref, sent_ref, slope_ref, pred_ref):
    parts, windows, _, bins = whole_ref.shape
    cores = 2
    places, per_place, tracks = target_ref.shape
    for w in range(windows):
        logits = jnp.zeros((bins, tracks), F32)
        for k in range(parts):
            core, x = divmod(k, parts // cores)
            logits += lax.dot_general(
                whole_ref[k, w], head_ref[x * cores + core], (((0,), (0,)), ((), ())), preferred_element_type=F32
            )
        low = jnp.exp(-jnp.abs(logits))
        pred_ref[w * bins : (w + 1) * bins, :] = (jnp.maximum(logits, 0.0) + jnp.log1p(low)).astype(BF16)
        slope_ref[w * bins : (w + 1) * bins, :] = jnp.where(logits >= 0, 1.0, low) / (1.0 + low)
    partial = jnp.dot(cover_ref[...], pred_ref[...], preferred_element_type=F32)
    partial = partial.reshape(places, per_place, tracks)
    sent_ref[:, :, :tracks] = partial.astype(BF16)
    sent_ref[:, :, tracks : 2 * tracks] = target_ref[...]
    sent_ref[:, :, 2 * tracks :] = jnp.zeros((places, per_place, LANES), BF16)
    total = jnp.sum(partial, axis=0)
    high, low = split(total + up(total))
    total = jnp.where(even_rows(total.shape), high, down(low)).astype(BF16)
    chunks = tracks // LANES
    for j in range(chunks):
        cut = slice(j * LANES, (j + 1) * LANES)
        for i in range(2):
            sent_ref[i * chunks + j, :, 2 * tracks :] = total[:, cut]
            sent_ref[(i + 2) * chunks + j, :, 2 * tracks :] = tsum_ref[:, cut]


def middle_kernel(at_ref, got_ref, sent_ref):
    places, per_place, width = got_ref.shape
    tracks = (width - LANES) // 2
    chunks = tracks // LANES
    got = jnp.sum(got_ref[...].astype(F32), axis=0)
    gene_pred = got[:, :tracks]
    gene_target = unspread(got[:, tracks : 2 * tracks])
    ratio = squared(gene_target / gene_pred).astype(BF16)
    sent_ref[:, :, :tracks] = jnp.broadcast_to(ratio[None], (places, per_place, tracks))
    fit = gene_target * jnp.log(gene_pred)
    fit = fit + down(fit)
    sums = got[:, 2 * tracks :]
    high, low = split(sums + up(sums))
    common = jnp.where(at_ref[0] % (2 * chunks) < chunks, high, low)
    even = even_rows(common.shape)
    common = jnp.where(even, common, 0.0)
    sent_ref[:, :, tracks:] = jnp.broadcast_to(common.astype(BF16)[None], (places, per_place, LANES))
    for j in range(chunks):
        cut = slice(j * LANES, (j + 1) * LANES)
        sent_ref[j * at_ref[1], :, tracks:] = jnp.where(even, common, fit[:, cut]).astype(BF16)


def backward_kernel(genes, block, at_ref, got_ref, turned_ref, slope_ref, whole_ref, sent_ref, total_ref, tsum_ref):
    places, per_place, width = got_ref.shape
    parts, windows, depth, bins = whole_ref.shape
    tracks = width - LANES
    chunks = tracks // LANES
    side = 8
    padded = sent_ref.shape[1]

    def joined(first):
        pieces = [
            got_ref[first + j, :, tracks:].astype(F32) + got_ref[first + chunks + j, :, tracks:].astype(F32)
            for j in range(chunks)
        ]
        row = jnp.concatenate(pieces, axis=1)
        return jnp.where(even_rows(row.shape), row, down(row))

    total = joined(0)
    target_sum = joined(2 * chunks)
    total_ref[...] = total
    tsum_ref[...] = target_sum
    scale = genes / target_sum
    level = scale * (0.2 + 0.8 * target_sum / total)
    ratio = rooted(got_ref[:, :, :tracks].astype(F32))
    gene_grad = (level[None] - scale[None] * ratio).reshape(places * per_place, tracks).astype(BF16)
    bin_grad = jnp.dot(turned_ref[...], gene_grad, preferred_element_type=F32)
    logit_grad = (bin_grad * slope_ref[...]).astype(BF16)

    fit = jnp.sum(got_ref[:, :, tracks:].astype(F32), axis=0)
    high, low = split(fit)
    row = lax.broadcasted_iota(jnp.int32, (padded, LANES), 0)
    holder = at_ref[2] == 1
    spare = []
    for w in range(windows):
        top = jnp.where(row == block, jnp.broadcast_to(high[2 * w + 1 : 2 * w + 2, :], row.shape), 0.0)
        top += jnp.where(row == block + 1, jnp.broadcast_to(low[2 * w + 1 : 2 * w + 2, :], row.shape), 0.0)
        spare.append(top)
    spare = jnp.where(holder, jnp.concatenate(spare, axis=1), 0.0)

    cores = 2
    for k in range(parts):
        core, x = divmod(k, parts // cores)
        lhs = jnp.concatenate([whole_ref[k, w] for w in range(windows)], axis=1)
        grad = jnp.dot(lhs, logit_grad, preferred_element_type=F32)
        for i in range(side):
            upper = x * cores + core
            place = upper * at_ref[3] + i * at_ref[4]
            sent_ref[place] = (grad[i * padded : (i + 1) * padded] + spare).astype(BF16)


def per_device(embeddings, head, exon_starts, exon_lengths, gene_owner, gene_targets):
    places = lax.axis_size(SEQ)
    place = lax.axis_index(SEQ)
    core = lax.axis_index("c")
    side = lax.axis_size("y")
    windows, bin_dev, channels_dev = embeddings.shape
    channels, tracks = head.shape
    genes = gene_owner.shape[1]
    capacity = gene_targets.shape[1]
    held = genes // places
    per_place = windows * held
    rows = places * per_place
    xs, cores = lax.axis_size("x"), lax.axis_size("c")
    parts = xs * cores
    block = channels // places
    padded = -(-block // 16) * 16
    blocks_dev = channels_dev // block
    depth = blocks_dev * padded
    chunks = tracks // LANES

    local = embeddings.transpose(0, 2, 1).reshape(windows, blocks_dev, block, bin_dev)
    local = jnp.pad(local, ((0, 0), (0, 0), (0, padded - block), (0, 0))).reshape(windows, depth, bin_dev)
    ours = gather(local, "x")
    whole = gather(ours, "c").reshape(parts, windows, depth, bin_dev)

    padded_head = jnp.pad(head.reshape(places, block, tracks), ((0, 0), (0, padded - block), (0, 0)))
    padded_head = padded_head.reshape(parts, depth, tracks)

    first = core == 0
    stride = jnp.where(first, 1, side)
    holder = jnp.where(first, place < chunks, (place % side == 0) & (place < chunks * side))
    at = jnp.stack(
        [place, stride, holder.astype(jnp.int32), jnp.where(first, side, 1), jnp.where(first, 1, side)]
    ).astype(jnp.int32)

    cover, turned = pl.pallas_call(
        lambda *refs: cover_kernel(windows, held, *refs),
        out_shape=[
            jax.ShapeDtypeStruct((rows, windows * bin_dev), BF16),
            jax.ShapeDtypeStruct((windows * bin_dev, rows), BF16),
        ],
        in_specs=[SMEM, VMEM, VMEM],
        out_specs=[VMEM, VMEM],
        name="cover",
    )(at, by_place(exon_starts, places).T, by_place(exon_lengths, places).T)

    row_window = (jnp.arange(rows, dtype=jnp.int32) // held) % windows
    in_window = row_window[:, None] == jnp.arange(windows)
    slot_row = by_place(slot_table(gene_owner, capacity), places)
    here = place * capacity + jnp.arange(capacity, dtype=jnp.int32)
    chosen = in_window[..., None] & (slot_row[:, None, None] == here)
    chosen = chosen.reshape(rows, windows * capacity)
    valid_here = jnp.any(chosen, axis=0).astype(F32)[:, None]
    targets_here = gene_targets.reshape(windows * capacity, tracks)
    targets_here = jnp.where(valid_here > 0, targets_here, 1.0)
    target_rows = jnp.dot(chosen.astype(BF16), spread(targets_here).astype(BF16), preferred_element_type=F32)
    target_rows = target_rows.astype(BF16).reshape(places, per_place, tracks)
    target_part = jnp.sum((targets_here * valid_here).reshape(windows, capacity, tracks), axis=1)
    high = lax.reduce_precision(target_part, 8, 7)
    tsum = jnp.stack([high, target_part - high], axis=1).reshape(per_place, tracks).astype(BF16)

    sent, slope = pl.pallas_call(
        forward_kernel,
        out_shape=[
            jax.ShapeDtypeStruct((places, per_place, 2 * tracks + LANES), BF16),
            jax.ShapeDtypeStruct((windows * bin_dev, tracks), F32),
        ],
        in_specs=[VMEM] * 5,
        out_specs=[VMEM] * 2,
        scratch_shapes=[pltpu.VMEM((windows * bin_dev, tracks), BF16)],
        name="forward",
    )(whole, padded_head, cover, target_rows, tsum)

    sent = pl.pallas_call(
        middle_kernel,
        out_shape=jax.ShapeDtypeStruct((places, per_place, tracks + LANES), BF16),
        in_specs=[SMEM, VMEM],
        out_specs=VMEM,
        name="middle",
    )(at, exchange(sent, SEQ))
    got = exchange(sent, SEQ)

    sent, total, target_sum = pl.pallas_call(
        lambda *refs: backward_kernel(genes, block, *refs),
        out_shape=[
            jax.ShapeDtypeStruct((places, padded, tracks), BF16),
            jax.ShapeDtypeStruct((per_place, tracks), F32),
            jax.ShapeDtypeStruct((per_place, tracks), F32),
        ],
        in_specs=[SMEM, VMEM, VMEM, VMEM, VMEM],
        out_specs=[VMEM] * 3,
        name="backward",
    )(at, got, turned, slope, whole)

    ahead, after = mixed_groups((side, places // side, xs, cores))
    summed = exchange(sent.reshape(side, side * padded, tracks), EVERY, ahead)
    summed = jnp.sum(summed.reshape(side, side, padded, tracks).astype(F32), axis=0)
    summed = exchange(summed, EVERY, after)
    grad_head = jnp.sum(summed[:, :block], axis=0)
    fit = jnp.sum(summed[:chunks, block:], axis=1).reshape(chunks, windows, LANES)
    fit = fit.transpose(1, 0, 2).reshape(windows, tracks)
    total = total.reshape(windows, held, tracks)[:, 0]
    target_sum = target_sum.reshape(windows, held, tracks)[:, 0]
    log_total = jnp.log(total)
    loss = (-fit + target_sum * log_total + 0.2 * (total - target_sum * log_total)) / target_sum

    ratios = got[:, :, :tracks].reshape(rows, tracks)
    back = lax.dot_general(chosen.astype(BF16), ratios, (((0,), (0,)), ((), ())), preferred_element_type=F32)
    gene_here = jnp.where(valid_here > 0, targets_here / rooted(jnp.where(valid_here > 0, back, 1.0)), 0.0)
    return (gene_here.reshape(gene_targets.shape), loss, grad_head)


def solution(mesh):
    shape = (8, 8, 4, 2)
    fine = Mesh(mesh.devices.reshape(shape), EVERY)
    return jax.shard_map(
        per_device,
        mesh=fine,
        in_specs=(P(None, SEQ, ("x", "c")), P(None, ("x", "c")), P(), P(), P(), P(None, SEQ, ("x", "c"))),
        out_specs=(P(None, SEQ, ("x", "c")), P(None, ("x", "c")), P(SEQ, ("x", "c"))),
        check_vma=False,
    )
```

```python
import jax
import jax.numpy as jnp
import numpy as np
from jax import lax
from jax.experimental import pallas as pl
from jax.experimental.pallas import tpu as pltpu
from jax.sharding import Mesh, PartitionSpec as P

SEQ = ("y", "z")
EVERY = ("y", "z", "x", "c")
F32 = jnp.float32
BF16 = jnp.bfloat16
MIDDLE = 28.28
LANES = 128
VMEM = pl.BlockSpec(memory_space=pltpu.VMEM)
SMEM = pl.BlockSpec(memory_space=pltpu.SMEM)
SMALL = pltpu.CompilerParams(vmem_limit_bytes=24 * 1024 * 1024)


def exchange(blocks, axes, groups=None):
    return lax.all_to_all(blocks, axes, split_axis=0, concat_axis=0, axis_index_groups=groups, tiled=True)


def mixed_groups(shape):
    ids = np.arange(int(np.prod(shape))).reshape(shape)
    ahead, after = [], []
    for x in range(shape[2]):
        for k in range(shape[0]):
            ahead += [ids[:, k, x, 0].tolist(), ids[k, :, x, 1].tolist()]
            after += [ids[k, :, x, 0].tolist(), ids[:, k, x, 1].tolist()]
    return ahead, after


def spread(counts):
    scaled = counts * (1.0 / MIDDLE)
    for _ in range(4):
        scaled = scaled * scaled
    return scaled


def unspread(coded):
    for _ in range(4):
        coded = jnp.sqrt(coded)
    return coded * MIDDLE


def squared(ratio):
    small = ratio < 2.0**63
    scaled = jnp.where(small, ratio, ratio * 2.0**-96)
    return jnp.where(small, scaled * scaled, -(scaled * scaled))


def rooted(coded):
    root = jnp.sqrt(jnp.abs(coded))
    return jnp.where(coded < 0, root * 2.0**96, root)


def split(values):
    high = values.astype(BF16).astype(F32)
    return high, values - high


def even_rows(shape):
    return lax.broadcasted_iota(jnp.int32, shape, 0) % 2 == 0


def up(values):
    return pltpu.roll(values, values.shape[0] - 1, 0)


def down(values):
    return pltpu.roll(values, 1, 0)


def slot_table(gene_owner, capacity):
    genes = gene_owner.shape[1]
    same = gene_owner[:, :, None] == gene_owner[:, None, :]
    earlier = jnp.arange(genes)[None, :] < jnp.arange(genes)[:, None]
    ahead = jnp.sum((same & earlier[None]).astype(jnp.int32), axis=2)
    return gene_owner * capacity + ahead


def by_place(table, places):
    windows, genes = table.shape[:2]
    held = genes // places
    parts = table.reshape((windows, places, held) + table.shape[2:])
    return jnp.moveaxis(parts, 1, 0).reshape((genes * windows,) + table.shape[2:])


def pack_kernel(block, padded, local_ref, packed_ref):
    copies, windows, depth, bins = packed_ref.shape
    for w in range(windows):
        rows = local_ref[w].astype(F32)
        gap = jnp.zeros((padded - block, bins), F32)
        pieces = []
        for i in range(depth // padded):
            pieces += [rows[i * block : (i + 1) * block], gap]
        rows = jnp.concatenate(pieces, axis=0).astype(BF16)
        for i in range(copies):
            packed_ref[i, w] = rows


def cover_kernel(windows, held, at_ref, starts_ref, lengths_ref, cover_ref, turned_ref):
    exons, rows = starts_ref.shape
    bins = cover_ref.shape[1] // windows
    position = lax.broadcasted_iota(jnp.int32, (bins, rows), 0) + at_ref[0] * bins
    base = jnp.zeros((bins, rows), F32)
    for e in range(exons):
        past = position - starts_ref[e : e + 1, :]
        base += jnp.where((past >= 0) & (past < lengths_ref[e : e + 1, :]), 1.0, 0.0)
    owner = (lax.broadcasted_iota(jnp.int32, (bins, rows), 1) // held) % windows
    for w in range(windows):
        mine = jnp.where(owner == w, base, 0.0)
        turned_ref[w * bins : (w + 1) * bins, :] = mine.astype(BF16)
        cover_ref[:, w * bins : (w + 1) * bins] = mine.T.astype(BF16)


def forward_kernel(at_ref, ours_ref, other_ref, head_ref, cover_ref, target_ref, tsum_ref, sent_ref, slope_ref, pred_ref):
    xs, windows, _, bins = ours_ref.shape
    core = at_ref[5]
    places, per_place, tracks = target_ref.shape
    for w in range(windows):
        logits = jnp.zeros((bins, tracks), F32)
        for x in range(xs):
            for ref, at in ((ours_ref, 2 * x + core), (other_ref, 2 * x + 1 - core)):
                logits += lax.dot_general(
                    ref[x, w], head_ref[at], (((0,), (0,)), ((), ())), preferred_element_type=F32
                )
        low = jnp.exp(-jnp.abs(logits))
        pred_ref[w * bins : (w + 1) * bins, :] = (jnp.maximum(logits, 0.0) + jnp.log1p(low)).astype(BF16)
        slope_ref[w * bins : (w + 1) * bins, :] = jnp.where(logits >= 0, 1.0, low) / (1.0 + low)
    partial = jnp.dot(cover_ref[...], pred_ref[...], preferred_element_type=F32)
    partial = partial.reshape(places, per_place, tracks)
    sent_ref[:, :, :tracks] = partial.astype(BF16)
    sent_ref[:, :, tracks : 2 * tracks] = target_ref[...]
    sent_ref[:, :, 2 * tracks :] = jnp.zeros((places, per_place, LANES), BF16)
    total = jnp.sum(partial, axis=0)
    high, low = split(total + up(total))
    total = jnp.where(even_rows(total.shape), high, down(low)).astype(BF16)
    chunks = tracks // LANES
    for j in range(chunks):
        cut = slice(j * LANES, (j + 1) * LANES)
        for i in range(2):
            sent_ref[i * chunks + j, :, 2 * tracks :] = total[:, cut]
            sent_ref[(i + 2) * chunks + j, :, 2 * tracks :] = tsum_ref[:, cut]


def middle_kernel(at_ref, got_ref, sent_ref):
    places, per_place, width = got_ref.shape
    tracks = (width - LANES) // 2
    chunks = tracks // LANES
    got = jnp.sum(got_ref[...].astype(F32), axis=0)
    gene_pred = got[:, :tracks]
    gene_target = unspread(got[:, tracks : 2 * tracks])
    ratio = squared(gene_target / gene_pred).astype(BF16)
    sent_ref[:, :, :tracks] = jnp.broadcast_to(ratio[None], (places, per_place, tracks))
    fit = gene_target * jnp.log(gene_pred)
    fit = fit + down(fit)
    sums = got[:, 2 * tracks :]
    high, low = split(sums + up(sums))
    common = jnp.where(at_ref[0] % (2 * chunks) < chunks, high, low)
    even = even_rows(common.shape)
    common = jnp.where(even, common, 0.0)
    sent_ref[:, :, tracks:] = jnp.broadcast_to(common.astype(BF16)[None], (places, per_place, LANES))
    for j in range(chunks):
        cut = slice(j * LANES, (j + 1) * LANES)
        sent_ref[j * at_ref[1], :, tracks:] = jnp.where(even, common, fit[:, cut]).astype(BF16)


def backward_kernel(
    genes, block, at_ref, got_ref, turned_ref, slope_ref, ours_ref, other_ref, sent_ref, total_ref, tsum_ref
):
    places, per_place, width = got_ref.shape
    xs, windows, depth, bins = ours_ref.shape
    tracks = width - LANES
    chunks = tracks // LANES
    side = 8
    padded = sent_ref.shape[1]

    def joined(first):
        pieces = [
            got_ref[first + j, :, tracks:].astype(F32) + got_ref[first + chunks + j, :, tracks:].astype(F32)
            for j in range(chunks)
        ]
        row = jnp.concatenate(pieces, axis=1)
        return jnp.where(even_rows(row.shape), row, down(row))

    total = joined(0)
    target_sum = joined(2 * chunks)
    total_ref[...] = total
    tsum_ref[...] = target_sum
    scale = genes / target_sum
    level = scale * (0.2 + 0.8 * target_sum / total)
    ratio = rooted(got_ref[:, :, :tracks].astype(F32))
    gene_grad = (level[None] - scale[None] * ratio).reshape(places * per_place, tracks).astype(BF16)
    bin_grad = jnp.dot(turned_ref[...], gene_grad, preferred_element_type=F32)
    logit_grad = (bin_grad * slope_ref[...]).astype(BF16)

    fit = jnp.sum(got_ref[:, :, tracks:].astype(F32), axis=0)
    high, low = split(fit)
    row = lax.broadcasted_iota(jnp.int32, (padded, LANES), 0)
    holder = at_ref[2] == 1
    spare = []
    for w in range(windows):
        top = jnp.where(row == block, jnp.broadcast_to(high[2 * w + 1 : 2 * w + 2, :], row.shape), 0.0)
        top += jnp.where(row == block + 1, jnp.broadcast_to(low[2 * w + 1 : 2 * w + 2, :], row.shape), 0.0)
        spare.append(top)
    spare = jnp.where(holder, jnp.concatenate(spare, axis=1), 0.0)

    core = at_ref[5]
    for x in range(xs):
        for ref, upper in ((ours_ref, 2 * x + core), (other_ref, 2 * x + 1 - core)):
            lhs = jnp.concatenate([ref[x, w] for w in range(windows)], axis=1)
            grad = jnp.dot(lhs, logit_grad, preferred_element_type=F32)
            for i in range(side):
                place = upper * at_ref[3] + i * at_ref[4]
                sent_ref[place] = (grad[i * padded : (i + 1) * padded] + spare).astype(BF16)


def per_device(embeddings, head, exon_starts, exon_lengths, gene_owner, gene_targets):
    places = lax.axis_size(SEQ)
    place = lax.axis_index(SEQ)
    core = lax.axis_index("c")
    side = lax.axis_size("y")
    windows, bin_dev, channels_dev = embeddings.shape
    channels, tracks = head.shape
    genes = gene_owner.shape[1]
    capacity = gene_targets.shape[1]
    held = genes // places
    per_place = windows * held
    rows = places * per_place
    xs, cores = lax.axis_size("x"), lax.axis_size("c")
    parts = xs * cores
    block = channels // places
    padded = -(-block // 16) * 16
    blocks_dev = channels_dev // block
    depth = blocks_dev * padded
    chunks = tracks // LANES

    packed = pl.pallas_call(
        lambda *refs: pack_kernel(block, padded, *refs),
        out_shape=jax.ShapeDtypeStruct((xs, windows, depth, bin_dev), BF16),
        in_specs=[VMEM],
        out_specs=VMEM,
        compiler_params=SMALL,
        name="pack",
    )(embeddings.transpose(0, 2, 1))
    ours = exchange(packed, "x")

    padded_head = jnp.pad(head.reshape(places, block, tracks), ((0, 0), (0, padded - block), (0, 0)))
    padded_head = padded_head.reshape(parts, depth, tracks)

    first = core == 0
    stride = jnp.where(first, 1, side)
    holder = jnp.where(first, place < chunks, (place % side == 0) & (place < chunks * side))
    at = jnp.stack(
        [place, stride, holder.astype(jnp.int32), jnp.where(first, side, 1), stride, core]
    ).astype(jnp.int32)

    starts, lengths = by_place(exon_starts, places).T, by_place(exon_lengths, places).T
    slot_row = by_place(slot_table(gene_owner, capacity), places)
    ours, starts, lengths, slot_row, padded_head = lax.optimization_barrier(
        (ours, starts, lengths, slot_row, padded_head)
    )
    other = lax.ppermute(ours, "c", [(0, 1), (1, 0)])

    cover, turned = pl.pallas_call(
        lambda *refs: cover_kernel(windows, held, *refs),
        out_shape=[
            jax.ShapeDtypeStruct((rows, windows * bin_dev), BF16),
            jax.ShapeDtypeStruct((windows * bin_dev, rows), BF16),
        ],
        in_specs=[SMEM, VMEM, VMEM],
        out_specs=[VMEM, VMEM],
        compiler_params=SMALL,
        name="cover",
    )(at, starts, lengths)

    row_window = (jnp.arange(rows, dtype=jnp.int32) // held) % windows
    in_window = row_window[:, None] == jnp.arange(windows)
    here = place * capacity + jnp.arange(capacity, dtype=jnp.int32)
    chosen = in_window[..., None] & (slot_row[:, None, None] == here)
    chosen = chosen.reshape(rows, windows * capacity)
    valid_here = jnp.any(chosen, axis=0).astype(F32)[:, None]
    targets_here = gene_targets.reshape(windows * capacity, tracks)
    targets_here = jnp.where(valid_here > 0, targets_here, 1.0)
    target_rows = jnp.dot(chosen.astype(BF16), spread(targets_here).astype(BF16), preferred_element_type=F32)
    target_rows = target_rows.astype(BF16).reshape(places, per_place, tracks)
    target_part = jnp.sum((targets_here * valid_here).reshape(windows, capacity, tracks), axis=1)
    high = lax.reduce_precision(target_part, 8, 7)
    tsum = jnp.stack([high, target_part - high], axis=1).reshape(per_place, tracks).astype(BF16)

    sent, slope = pl.pallas_call(
        forward_kernel,
        out_shape=[
            jax.ShapeDtypeStruct((places, per_place, 2 * tracks + LANES), BF16),
            jax.ShapeDtypeStruct((windows * bin_dev, tracks), F32),
        ],
        in_specs=[SMEM] + [VMEM] * 6,
        out_specs=[VMEM] * 2,
        scratch_shapes=[pltpu.VMEM((windows * bin_dev, tracks), BF16)],
        compiler_params=SMALL,
        name="forward",
    )(at, ours, other, padded_head, cover, target_rows, tsum)

    sent = pl.pallas_call(
        middle_kernel,
        out_shape=jax.ShapeDtypeStruct((places, per_place, tracks + LANES), BF16),
        in_specs=[SMEM, VMEM],
        out_specs=VMEM,
        compiler_params=SMALL,
        name="middle",
    )(at, exchange(sent, SEQ))
    got = exchange(sent, SEQ)

    sent, total, target_sum = pl.pallas_call(
        lambda *refs: backward_kernel(genes, block, *refs),
        out_shape=[
            jax.ShapeDtypeStruct((places, padded, tracks), BF16),
            jax.ShapeDtypeStruct((per_place, tracks), F32),
            jax.ShapeDtypeStruct((per_place, tracks), F32),
        ],
        in_specs=[SMEM] + [VMEM] * 5,
        out_specs=[VMEM] * 3,
        compiler_params=SMALL,
        name="backward",
    )(at, got, turned, slope, ours, other)

    ahead, after = mixed_groups((side, places // side, xs, cores))
    summed = exchange(sent.reshape(side, side * padded, tracks), EVERY, ahead)
    summed = jnp.sum(summed.reshape(side, side, padded, tracks).astype(F32), axis=0)
    is_grad = (jnp.arange(padded) < block)[:, None]
    summed = jnp.where(is_grad, summed * jnp.abs(summed), summed).astype(BF16)
    summed = exchange(summed, EVERY, after).astype(F32)
    grads = summed[:, :block]
    root = jnp.sqrt(jnp.abs(grads))
    grad_head = jnp.sum(jnp.where(grads < 0, -root, root), axis=0)
    fit = jnp.sum(summed[:chunks, block:], axis=1).reshape(chunks, windows, LANES)
    fit = fit.transpose(1, 0, 2).reshape(windows, tracks)
    total = total.reshape(windows, held, tracks)[:, 0]
    target_sum = target_sum.reshape(windows, held, tracks)[:, 0]
    log_total = jnp.log(total)
    loss = (-fit + target_sum * log_total + 0.2 * (total - target_sum * log_total)) / target_sum

    ratios = got[:, :, :tracks].reshape(rows, tracks)
    back = lax.dot_general(chosen.astype(BF16), ratios, (((0,), (0,)), ((), ())), preferred_element_type=F32)
    gene_here = jnp.where(valid_here > 0, targets_here / rooted(jnp.where(valid_here > 0, back, 1.0)), 0.0)
    return (gene_here.reshape(gene_targets.shape), loss, grad_head)


def solution(mesh):
    shape = (8, 8, 4, 2)
    fine = Mesh(mesh.devices.reshape(shape), EVERY)
    return jax.shard_map(
        per_device,
        mesh=fine,
        in_specs=(P(None, SEQ, ("x", "c")), P(None, ("x", "c")), P(), P(), P(), P(None, SEQ, ("x", "c"))),
        out_specs=(P(None, SEQ, ("x", "c")), P(None, ("x", "c")), P(SEQ, ("x", "c"))),
        check_vma=False,
    )
```

```python
import jax
import jax.numpy as jnp
import numpy as np
from jax import lax
from jax.experimental import pallas as pl
from jax.experimental.pallas import tpu as pltpu
from jax.sharding import Mesh, PartitionSpec as P

SEQ = ("y", "z")
EVERY = ("y", "z", "x", "c")
F32 = jnp.float32
BF16 = jnp.bfloat16
MIDDLE = 28.28
LANES = 128
VMEM = pl.BlockSpec(memory_space=pltpu.VMEM)
SMEM = pl.BlockSpec(memory_space=pltpu.SMEM)
SMALL = pltpu.CompilerParams(vmem_limit_bytes=16 * 1024 * 1024)


def exchange(blocks, axes, groups=None):
    return lax.all_to_all(blocks, axes, split_axis=0, concat_axis=0, axis_index_groups=groups, tiled=True)


def mixed_groups(shape):
    ids = np.arange(int(np.prod(shape))).reshape(shape)
    ahead, after = [], []
    for x in range(shape[2]):
        for k in range(shape[0]):
            ahead += [ids[:, k, x, 0].tolist(), ids[k, :, x, 1].tolist()]
            after += [ids[k, :, x, 0].tolist(), ids[:, k, x, 1].tolist()]
    return ahead, after


def spread(counts):
    scaled = counts * (1.0 / MIDDLE)
    for _ in range(4):
        scaled = scaled * scaled
    return scaled


def unspread(coded):
    for _ in range(4):
        coded = jnp.sqrt(coded)
    return coded * MIDDLE


def squared(ratio):
    small = ratio < 2.0**63
    scaled = jnp.where(small, ratio, ratio * 2.0**-96)
    return jnp.where(small, scaled * scaled, -(scaled * scaled))


def rooted(coded):
    root = jnp.sqrt(jnp.abs(coded))
    return jnp.where(coded < 0, root * 2.0**96, root)


def split(values):
    high = values.astype(BF16).astype(F32)
    return high, values - high


def even_rows(shape):
    return lax.broadcasted_iota(jnp.int32, shape, 0) % 2 == 0


def up(values):
    return pltpu.roll(values, values.shape[0] - 1, 0)


def down(values):
    return pltpu.roll(values, 1, 0)


def pack_kernel(block, padded, local_ref, packed_ref):
    copies, windows, depth, bins = packed_ref.shape
    for w in range(windows):
        rows = local_ref[w].astype(F32)
        gap = jnp.zeros((padded - block, bins), F32)
        pieces = []
        for i in range(depth // padded):
            pieces += [rows[i * block : (i + 1) * block], gap]
        rows = jnp.concatenate(pieces, axis=0).astype(BF16)
        for i in range(copies):
            packed_ref[i, w] = rows


def plan_kernel(
    places, at_ref, owner_ref, starts_ref, lengths_ref, counts_ref, cover_ref, turned_ref, target_ref, tsum_ref, mine_ref, from_ref
):
    windows, genes = owner_ref.shape
    exons = starts_ref.shape[1]
    capacity, tracks = counts_ref.shape[1:]
    held = genes // places
    per_place = windows * held
    rows = places * per_place
    bins = cover_ref.shape[1] // windows
    width = target_ref.shape[2]
    place = at_ref[0]
    square = (genes, genes)
    earlier = lax.broadcasted_iota(jnp.int32, square, 1) < lax.broadcasted_iota(jnp.int32, square, 0)
    position = lax.broadcasted_iota(jnp.int32, (bins, genes), 0) + place * bins
    lane = lax.broadcasted_iota(jnp.int32, (genes, rows), 1)
    targets = jnp.zeros((rows, width), F32)
    tsum, sources = [], []
    for w in range(windows):
        other = jnp.broadcast_to(owner_ref[w : w + 1, :].astype(F32), square)
        own = other.T
        ahead = jnp.where((other == own) & earlier, 1.0, 0.0)
        rank = jnp.sum(ahead, axis=1, keepdims=True)
        at = jnp.sum(jnp.where(other < own, 1.0, ahead), axis=1, keepdims=True).astype(jnp.int32)
        turn = at // places
        holder = at - turn * places
        first = holder * per_place + w * held
        spot = jnp.where(first + turn == lane, 1.0, 0.0).astype(BF16)

        base = jnp.zeros((bins, genes), F32)
        for e in range(exons):
            past = position - starts_ref[w, e : e + 1, :]
            base += jnp.where((past >= 0) & (past < lengths_ref[w, e : e + 1, :]), 1.0, 0.0)
        turned = jnp.dot(base.astype(BF16), spot, preferred_element_type=F32)
        turned_ref[w * bins : (w + 1) * bins, :] = turned.astype(BF16)
        cover_ref[:, w * bins : (w + 1) * bins] = turned.T.astype(BF16)

        owned = own[:, :1] == place.astype(F32)
        coded = jnp.zeros((genes, tracks), F32)
        total = jnp.zeros((1, tracks), F32)
        for k in range(capacity):
            here = owned & (rank == k)
            count = counts_ref[w, k : k + 1, :]
            held_here = jnp.sum(jnp.where(here, 1.0, 0.0), axis=0, keepdims=True) > 0
            count = jnp.where(jnp.broadcast_to(held_here, count.shape), count, 1.0)
            coded += jnp.where(jnp.broadcast_to(here, coded.shape), jnp.broadcast_to(spread(count), coded.shape), 0.0)
            total += jnp.where(jnp.broadcast_to(held_here, count.shape), count, 0.0)
            row = jnp.where(jnp.broadcast_to(here, lane.shape), spot.astype(F32), 0.0)
            mine_ref[w * capacity + k : w * capacity + k + 1, :] = jnp.sum(row, axis=0, keepdims=True)
        coded = coded.astype(BF16)
        for h in range(held):
            goes = jnp.where(first + h == lane, 1.0, 0.0).astype(BF16)
            targets += lax.dot_general(
                goes, coded[:, h * width : (h + 1) * width], (((0,), (0,)), ((), ())), preferred_element_type=F32
            )
            match = jnp.where(at == place + h * places, own[:, :1], 0.0)
            sources.append(jnp.sum(match, axis=0, keepdims=True))
        tsum += list(split(total))
    target_ref[...] = targets.reshape(places, per_place, width).astype(BF16)
    tsum_ref[...] = jnp.concatenate(tsum, axis=0).astype(BF16)
    from_ref[...] = jnp.broadcast_to(jnp.concatenate(sources, axis=0), from_ref.shape).astype(jnp.int32)


def forward_kernel(at_ref, ours_ref, other_ref, head_ref, cover_ref, target_ref, tsum_ref, sent_ref, slope_ref, pred_ref):
    xs, windows, _, bins = ours_ref.shape
    core = at_ref[5]
    places, per_place, extra = target_ref.shape
    tracks = slope_ref.shape[1]
    side = tracks + extra
    for w in range(windows):
        logits = jnp.zeros((bins, tracks), F32)
        for x in range(xs):
            for ref, at in ((ours_ref, 2 * x + core), (other_ref, 2 * x + 1 - core)):
                logits += lax.dot_general(
                    ref[x, w], head_ref[at], (((0,), (0,)), ((), ())), preferred_element_type=F32
                )
        low = jnp.exp(-jnp.abs(logits))
        pred_ref[w * bins : (w + 1) * bins, :] = (jnp.maximum(logits, 0.0) + jnp.log1p(low)).astype(BF16)
        slope_ref[w * bins : (w + 1) * bins, :] = jnp.where(logits >= 0, 1.0, low) / (1.0 + low)
    partial = jnp.dot(cover_ref[...], pred_ref[...], preferred_element_type=F32)
    partial = partial.reshape(places, per_place, tracks)
    sent_ref[:, :, :tracks] = partial.astype(BF16)
    sent_ref[:, :, tracks:side] = target_ref[...]
    sent_ref[:, :, side:] = jnp.zeros((places, per_place, LANES), BF16)
    total = jnp.sum(partial, axis=0)
    high, low = split(total + up(total))
    total = jnp.where(even_rows(total.shape), high, down(low)).astype(BF16)
    chunks = tracks // LANES
    for j in range(chunks):
        cut = slice(j * LANES, (j + 1) * LANES)
        for i in range(2):
            sent_ref[i * chunks + j, :, side:] = total[:, cut]
            sent_ref[(i + 2) * chunks + j, :, side:] = tsum_ref[:, cut]


def middle_kernel(held, at_ref, from_ref, got_ref, sent_ref):
    places, per_place, width = got_ref.shape
    tracks = sent_ref.shape[2] - LANES
    chunks = tracks // LANES
    side = width - LANES
    gene_pred = jnp.sum(got_ref[:, :, :tracks].astype(F32), axis=0)
    sums = jnp.sum(got_ref[:, :, side:].astype(F32), axis=0)
    pieces = []
    for row in range(per_place):
        w = row // held
        block = got_ref[from_ref[row], :, tracks:side].astype(F32)
        pieces.append(jnp.concatenate([block[w * held + h : w * held + h + 1] for h in range(held)], axis=1))
    gene_target = unspread(jnp.concatenate(pieces, axis=0))
    ratio = squared(gene_target / gene_pred).astype(BF16)
    sent_ref[:, :, :tracks] = jnp.broadcast_to(ratio[None], (places, per_place, tracks))
    fit = gene_target * jnp.log(gene_pred)
    fit = fit + down(fit)
    high, low = split(sums + up(sums))
    common = jnp.where(at_ref[0] % (2 * chunks) < chunks, high, low)
    even = even_rows(common.shape)
    common = jnp.where(even, common, 0.0)
    sent_ref[:, :, tracks:] = jnp.broadcast_to(common.astype(BF16)[None], (places, per_place, LANES))
    for j in range(chunks):
        cut = slice(j * LANES, (j + 1) * LANES)
        sent_ref[j * at_ref[1], :, tracks:] = jnp.where(even, common, fit[:, cut]).astype(BF16)


def backward_kernel(
    genes, block, at_ref, got_ref, turned_ref, slope_ref, ours_ref, other_ref, sent_ref, total_ref, tsum_ref
):
    places, per_place, width = got_ref.shape
    xs, windows, depth, bins = ours_ref.shape
    tracks = width - LANES
    chunks = tracks // LANES
    side = 8
    padded = sent_ref.shape[1]

    def joined(first):
        pieces = [
            got_ref[first + j, :, tracks:].astype(F32) + got_ref[first + chunks + j, :, tracks:].astype(F32)
            for j in range(chunks)
        ]
        row = jnp.concatenate(pieces, axis=1)
        return jnp.where(even_rows(row.shape), row, down(row))

    total = joined(0)
    target_sum = joined(2 * chunks)
    total_ref[...] = total
    tsum_ref[...] = target_sum
    scale = genes / target_sum
    level = scale * (0.2 + 0.8 * target_sum / total)
    ratio = rooted(got_ref[:, :, :tracks].astype(F32))
    gene_grad = (level[None] - scale[None] * ratio).reshape(places * per_place, tracks).astype(BF16)
    bin_grad = jnp.dot(turned_ref[...], gene_grad, preferred_element_type=F32)
    logit_grad = (bin_grad * slope_ref[...]).astype(BF16)

    fit = jnp.sum(got_ref[:, :, tracks:].astype(F32), axis=0)
    high, low = split(fit)
    row = lax.broadcasted_iota(jnp.int32, (padded, LANES), 0)
    holder = at_ref[2] == 1
    spare = []
    for w in range(windows):
        top = jnp.where(row == block, jnp.broadcast_to(high[2 * w + 1 : 2 * w + 2, :], row.shape), 0.0)
        top += jnp.where(row == block + 1, jnp.broadcast_to(low[2 * w + 1 : 2 * w + 2, :], row.shape), 0.0)
        spare.append(top)
    spare = jnp.where(holder, jnp.concatenate(spare, axis=1), 0.0)

    core = at_ref[5]
    for x in range(xs):
        for ref, upper in ((ours_ref, 2 * x + core), (other_ref, 2 * x + 1 - core)):
            lhs = jnp.concatenate([ref[x, w] for w in range(windows)], axis=1)
            grad = jnp.dot(lhs, logit_grad, preferred_element_type=F32)
            for i in range(side):
                place = upper * at_ref[3] + i * at_ref[4]
                sent_ref[place] = (grad[i * padded : (i + 1) * padded] + spare).astype(BF16)


def fold_kernel(block, got_ref, sent_ref):
    for i in range(sent_ref.shape[0]):
        total = got_ref[0, i].astype(F32)
        for j in range(1, got_ref.shape[0]):
            total += got_ref[j, i].astype(F32)
        row = lax.broadcasted_iota(jnp.int32, total.shape, 0)
        sent_ref[i] = jnp.where(row < block, total * jnp.abs(total), total).astype(BF16)


def per_device(embeddings, head, exon_starts, exon_lengths, gene_owner, gene_targets):
    places = lax.axis_size(SEQ)
    place = lax.axis_index(SEQ)
    core = lax.axis_index("c")
    side = lax.axis_size("y")
    windows, bin_dev, channels_dev = embeddings.shape
    channels, tracks = head.shape
    genes = gene_owner.shape[1]
    capacity = gene_targets.shape[1]
    held = genes // places
    per_place = windows * held
    rows = places * per_place
    xs, cores = lax.axis_size("x"), lax.axis_size("c")
    parts = xs * cores
    block = channels // places
    padded = -(-block // 16) * 16
    blocks_dev = channels_dev // block
    depth = blocks_dev * padded
    chunks = tracks // LANES

    packed = pl.pallas_call(
        lambda *refs: pack_kernel(block, padded, *refs),
        out_shape=jax.ShapeDtypeStruct((xs, windows, depth, bin_dev), BF16),
        in_specs=[VMEM],
        out_specs=VMEM,
        compiler_params=SMALL,
        name="pack",
    )(embeddings.transpose(0, 2, 1))
    ours = exchange(packed, "x")

    padded_head = jnp.pad(head.reshape(places, block, tracks), ((0, 0), (0, padded - block), (0, 0)))
    padded_head = padded_head.reshape(parts, depth, tracks)

    first = core == 0
    stride = jnp.where(first, 1, side)
    holder = jnp.where(first, place < chunks, (place % side == 0) & (place < chunks * side))
    at = jnp.stack(
        [place, stride, holder.astype(jnp.int32), jnp.where(first, side, 1), stride, core]
    ).astype(jnp.int32)

    extra = windows * tracks // per_place
    plan = pl.pallas_call(
        lambda *refs: plan_kernel(places, *refs),
        out_shape=[
            jax.ShapeDtypeStruct((rows, windows * bin_dev), BF16),
            jax.ShapeDtypeStruct((windows * bin_dev, rows), BF16),
            jax.ShapeDtypeStruct((places, per_place, extra), BF16),
            jax.ShapeDtypeStruct((per_place, tracks), BF16),
            jax.ShapeDtypeStruct((windows * capacity, rows), F32),
            jax.ShapeDtypeStruct((per_place, LANES), jnp.int32),
        ],
        in_specs=[SMEM] + [VMEM] * 4,
        out_specs=[VMEM] * 6,
        compiler_params=SMALL,
        name="plan",
    )(at, gene_owner, exon_starts.transpose(0, 2, 1), exon_lengths.transpose(0, 2, 1), gene_targets)
    came_from = plan[-1][:, 0]
    ours, padded_head, came_from, plan = lax.optimization_barrier((ours, padded_head, came_from, tuple(plan[:-1])))
    cover, turned, target_rows, tsum, mine = plan
    other = lax.ppermute(ours, "c", [(0, 1), (1, 0)])

    sent, slope = pl.pallas_call(
        forward_kernel,
        out_shape=[
            jax.ShapeDtypeStruct((places, per_place, tracks + extra + LANES), BF16),
            jax.ShapeDtypeStruct((windows * bin_dev, tracks), F32),
        ],
        in_specs=[SMEM] + [VMEM] * 6,
        out_specs=[VMEM] * 2,
        scratch_shapes=[pltpu.VMEM((windows * bin_dev, tracks), BF16)],
        compiler_params=SMALL,
        name="forward",
    )(at, ours, other, padded_head, cover, target_rows, tsum)

    sent = pl.pallas_call(
        lambda *refs: middle_kernel(held, *refs),
        out_shape=jax.ShapeDtypeStruct((places, per_place, tracks + LANES), BF16),
        in_specs=[SMEM, SMEM, VMEM],
        out_specs=VMEM,
        compiler_params=SMALL,
        name="middle",
    )(at, came_from, exchange(sent, SEQ))
    got = exchange(sent, SEQ)

    sent, total, target_sum = pl.pallas_call(
        lambda *refs: backward_kernel(genes, block, *refs),
        out_shape=[
            jax.ShapeDtypeStruct((places, padded, tracks), BF16),
            jax.ShapeDtypeStruct((per_place, tracks), F32),
            jax.ShapeDtypeStruct((per_place, tracks), F32),
        ],
        in_specs=[SMEM] + [VMEM] * 5,
        out_specs=[VMEM] * 3,
        compiler_params=SMALL,
        name="backward",
    )(at, got, turned, slope, ours, other)

    ahead, after = mixed_groups((side, places // side, xs, cores))
    summed = exchange(sent.reshape(side, side * padded, tracks), EVERY, ahead)
    summed = pl.pallas_call(
        lambda *refs: fold_kernel(block, *refs),
        out_shape=jax.ShapeDtypeStruct((side, padded, tracks), BF16),
        in_specs=[VMEM],
        out_specs=VMEM,
        compiler_params=SMALL,
        name="fold",
    )(summed.reshape(side, side, padded, tracks))
    summed, got, mine, total, target_sum, gene_targets = lax.optimization_barrier(
        (summed, got, mine, total, target_sum, gene_targets)
    )
    summed = exchange(summed, EVERY, after).astype(F32)
    grads = summed[:, :block]
    root = jnp.sqrt(jnp.abs(grads))
    grad_head = jnp.sum(jnp.where(grads < 0, -root, root), axis=0)
    fit = jnp.sum(summed[:chunks, block:], axis=1).reshape(chunks, windows, LANES)
    fit = fit.transpose(1, 0, 2).reshape(windows, tracks)
    total = total.reshape(windows, held, tracks)[:, 0]
    target_sum = target_sum.reshape(windows, held, tracks)[:, 0]
    log_total = jnp.log(total)
    loss = (-fit + target_sum * log_total + 0.2 * (total - target_sum * log_total)) / target_sum

    ratios = got[:, :, :tracks].reshape(rows, tracks)
    back = jnp.dot(mine.astype(BF16), ratios, preferred_element_type=F32)
    valid = jnp.sum(mine, axis=1, keepdims=True) > 0
    targets_here = gene_targets.reshape(windows * capacity, tracks)
    gene_here = jnp.where(valid, targets_here / rooted(jnp.where(valid, back, 1.0)), 0.0)
    return (gene_here.reshape(gene_targets.shape), loss, grad_head)


def solution(mesh):
    shape = (8, 8, 4, 2)
    fine = Mesh(mesh.devices.reshape(shape), EVERY)
    return jax.shard_map(
        per_device,
        mesh=fine,
        in_specs=(P(None, SEQ, ("x", "c")), P(None, ("x", "c")), P(), P(), P(), P(None, SEQ, ("x", "c"))),
        out_specs=(P(None, SEQ, ("x", "c")), P(None, ("x", "c")), P(SEQ, ("x", "c"))),
        check_vma=False,
    )
```

```python
import jax
import jax.numpy as jnp
import numpy as np
from jax import lax
from jax.experimental import pallas as pl
from jax.experimental.pallas import tpu as pltpu
from jax.sharding import Mesh, PartitionSpec as P

SEQ = ("y", "z")
EVERY = ("y", "z", "x", "c")
F32 = jnp.float32
BF16 = jnp.bfloat16
MIDDLE = 28.28
VMEM = pl.BlockSpec(memory_space=pltpu.VMEM)
SMEM = pl.BlockSpec(memory_space=pltpu.SMEM)
SMALL = pltpu.CompilerParams(vmem_limit_bytes=16 * 1024 * 1024)


def exchange(blocks, axes, groups=None):
    return lax.all_to_all(blocks, axes, split_axis=0, concat_axis=0, axis_index_groups=groups, tiled=True)


def mixed_groups(shape):
    ids = np.arange(int(np.prod(shape))).reshape(shape)
    ahead, after = [], []
    for x in range(shape[2]):
        for k in range(shape[0]):
            ahead += [ids[:, k, x, 0].tolist(), ids[k, :, x, 1].tolist()]
            after += [ids[k, :, x, 0].tolist(), ids[:, k, x, 1].tolist()]
    return ahead, after


def spread(counts):
    scaled = counts * (1.0 / MIDDLE)
    for _ in range(4):
        scaled = scaled * scaled
    return scaled


def unspread(coded):
    for _ in range(4):
        coded = jnp.sqrt(coded)
    return coded * MIDDLE


def squared(ratio):
    small = ratio < 2.0**63
    scaled = jnp.where(small, ratio, ratio * 2.0**-96)
    return jnp.where(small, scaled * scaled, -(scaled * scaled))


def rooted(coded):
    root = jnp.sqrt(jnp.abs(coded))
    return jnp.where(coded < 0, root * 2.0**96, root)


def split(values):
    high = values.astype(BF16).astype(F32)
    return high, values - high


def packed_sum(partial):
    tiny = partial < 2.0**-40
    scaled = jnp.where(tiny, partial * 2.0**80, partial)
    return jnp.where(tiny, -(scaled * scaled), scaled * scaled)


def unpacked_sum(coded):
    root = jnp.sqrt(jnp.abs(coded))
    return jnp.where(coded < 0, root * 2.0**-80, root)


def pack_kernel(block, padded, local_ref, packed_ref):
    copies, windows, depth, bins = packed_ref.shape
    for w in range(windows):
        rows = local_ref[w].astype(F32)
        gap = jnp.zeros((padded - block, bins), F32)
        pieces = []
        for i in range(depth // padded):
            pieces += [rows[i * block : (i + 1) * block], gap]
        rows = jnp.concatenate(pieces, axis=0).astype(BF16)
        for i in range(copies):
            packed_ref[i, w] = rows


def plan_kernel(
    places, at_ref, owner_ref, starts_ref, lengths_ref, counts_ref, cover_ref, turned_ref, target_ref, pick_ref, mine_ref
):
    windows, genes = owner_ref.shape
    exons = starts_ref.shape[1]
    capacity, tracks = counts_ref.shape[1:]
    held = genes // places
    side = target_ref.shape[0]
    sent_rows = target_ref.shape[1]
    rows, width = cover_ref.shape
    bins = width // windows
    set_rows, sources = pick_ref.shape
    window_rows = set_rows // windows
    place, core, axis = at_ref[0], at_ref[1], at_ref[2]
    square = (genes, genes)
    earlier = lax.broadcasted_iota(jnp.int32, square, 1) < lax.broadcasted_iota(jnp.int32, square, 0)
    position = lax.broadcasted_iota(jnp.int32, (bins, genes), 0) + place * bins
    lane = lax.broadcasted_iota(jnp.int32, (genes, rows), 1)
    targets = jnp.zeros((side * sent_rows, tracks), F32)
    pick = jnp.zeros((set_rows, sources), F32)
    across = (((0,), (0,)), ((), ()))
    for w in range(windows):
        other = jnp.broadcast_to(owner_ref[w : w + 1, :].astype(F32), square)
        own = other.T
        ahead = jnp.where((other == own) & earlier, 1.0, 0.0)
        rank = jnp.sum(ahead, axis=1, keepdims=True)
        at = jnp.sum(jnp.where(other < own, 1.0, ahead), axis=1, keepdims=True).astype(jnp.int32)
        turn = at // places
        place_of = at - turn * places
        high = place_of // side
        part = place_of - high * side
        row = w * window_rows + high * held + turn
        spot = jnp.where(part * set_rows + row == lane, 1.0, 0.0)

        base = jnp.zeros((bins, genes), F32)
        for e in range(exons):
            past = position - starts_ref[w, e : e + 1, :]
            base += jnp.where((past >= 0) & (past < lengths_ref[w, e : e + 1, :]), 1.0, 0.0)
        turned = jnp.dot(base.astype(BF16), spot.astype(BF16), preferred_element_type=F32)
        turned_ref[w * bins : (w + 1) * bins, :] = turned.astype(BF16)
        cover_ref[:, w * bins : (w + 1) * bins] = turned.T.astype(BF16)

        owner = own[:, :1].astype(jnp.int32)
        owner_high = owner // side
        owner_low = owner - owner_high * side
        first = jnp.where(core == 0, owner_high, owner_low)
        second = jnp.where(core == 0, owner_low, owner_high)
        source = second * (sources // side) + first * windows + w
        here = jnp.where((part == axis) & (row == lane[:, :set_rows]), 1.0, 0.0).astype(BF16)
        origin = jnp.where(source == lane[:, :sources], 1.0, 0.0).astype(BF16)
        pick += lax.dot_general(here, origin, across, preferred_element_type=F32)

        owned = owner == place
        coded = jnp.zeros((genes, tracks), F32)
        for k in range(capacity):
            slot = owned & (rank == k)
            filled = jnp.sum(jnp.where(slot, 1.0, 0.0), axis=0, keepdims=True) > 0
            count = counts_ref[w, k : k + 1, :]
            count = spread(jnp.where(jnp.broadcast_to(filled, count.shape), count, 1.0))
            coded += jnp.where(jnp.broadcast_to(slot, coded.shape), jnp.broadcast_to(count, coded.shape), 0.0)
            mark = jnp.where(jnp.broadcast_to(slot, lane.shape), spot, 0.0)
            mine_ref[w * capacity + k : w * capacity + k + 1, :] = jnp.sum(mark, axis=0, keepdims=True)
        goes = jnp.where(part * sent_rows + w == lane[:, : side * sent_rows], 1.0, 0.0).astype(BF16)
        targets += lax.dot_general(goes, coded.astype(BF16), across, preferred_element_type=F32)
    target_ref[...] = targets.reshape(side, sent_rows, tracks).astype(BF16)
    pick_ref[...] = pick.astype(BF16)


def forward_kernel(at_ref, ours_ref, other_ref, head_ref, cover_ref, target_ref, sent_ref, slope_ref, pred_ref):
    xs, windows, _, bins = ours_ref.shape
    core = at_ref[1]
    side, sent_rows, tracks = sent_ref.shape
    set_rows = sent_rows - target_ref.shape[1]
    for w in range(windows):
        logits = jnp.zeros((bins, tracks), F32)
        for x in range(xs):
            for ref, at in ((ours_ref, 2 * x + core), (other_ref, 2 * x + 1 - core)):
                logits += lax.dot_general(
                    ref[x, w], head_ref[at], (((0,), (0,)), ((), ())), preferred_element_type=F32
                )
        low = jnp.exp(-jnp.abs(logits))
        pred_ref[w * bins : (w + 1) * bins, :] = (jnp.maximum(logits, 0.0) + jnp.log1p(low)).astype(BF16)
        slope_ref[w * bins : (w + 1) * bins, :] = jnp.where(logits >= 0, 1.0, low) / (1.0 + low)
    partial = jnp.dot(cover_ref[...], pred_ref[...], preferred_element_type=F32)
    sent_ref[:, :set_rows, :] = packed_sum(partial).reshape(side, set_rows, tracks).astype(BF16)
    sent_ref[:, set_rows:, :] = target_ref[...]


def second_kernel(windows, got_ref, sent_ref):
    side, got_rows, tracks = got_ref.shape
    set_rows = got_rows - 2 * windows
    total = unpacked_sum(got_ref[0, :set_rows, :].astype(F32))
    for i in range(1, side):
        total += unpacked_sum(got_ref[i, :set_rows, :].astype(F32))
    pieces = [packed_sum(total)]
    for i in range(0, side, 2):
        upper = got_ref[i, set_rows:, :].astype(F32)
        pieces.append(upper + pltpu.roll(got_ref[i + 1, set_rows:, :].astype(F32), windows, 0))
    block = jnp.concatenate(pieces, axis=0).astype(BF16)
    for i in range(side):
        sent_ref[i] = block


def third_kernel(windows, got_ref, pick_ref, sent_ref):
    side, got_rows, tracks = got_ref.shape
    set_rows, sources = pick_ref.shape
    gene_pred = unpacked_sum(got_ref[0, :set_rows, :].astype(F32))
    for i in range(1, side):
        gene_pred += unpacked_sum(got_ref[i, :set_rows, :].astype(F32))
    rows = got_ref[:, set_rows:, :].astype(F32).reshape(sources, tracks).astype(BF16)
    gene_target = unspread(jnp.dot(pick_ref[...], rows, preferred_element_type=F32))
    pieces = [squared(gene_target / gene_pred)]
    for values in (gene_pred, gene_target, gene_target * jnp.log(gene_pred)):
        pieces += split(jnp.sum(values.reshape(windows, set_rows // windows, tracks), axis=1))
    block = jnp.concatenate(pieces, axis=0).astype(BF16)
    for i in range(side):
        sent_ref[i] = block


def backward_kernel(
    genes, at_ref, got_ref, turned_ref, slope_ref, ours_ref, other_ref, sent_ref, loss_ref
):
    side, got_rows, tracks = got_ref.shape
    xs, windows, depth, bins = ours_ref.shape
    set_rows = got_rows - 6 * windows
    window_rows = set_rows // windows
    padded = sent_ref.shape[1]
    sums = jnp.sum(got_ref[:, set_rows:, :].astype(F32), axis=0)
    total, target_sum, fit = [
        sums[2 * i * windows : (2 * i + 1) * windows] + sums[(2 * i + 1) * windows : (2 * i + 2) * windows]
        for i in range(3)
    ]
    log_total = jnp.log(total)
    loss_ref[...] = (-fit + target_sum * log_total + 0.2 * (total - target_sum * log_total)) / target_sum
    scale = genes / target_sum
    level = scale * (0.2 + 0.8 * target_sum / total)
    grads = []
    for w in range(windows):
        ratio = rooted(got_ref[:, w * window_rows : (w + 1) * window_rows, :].astype(F32))
        grads.append(level[w : w + 1][None] - scale[w : w + 1][None] * ratio)
    gene_grad = jnp.concatenate(grads, axis=1).reshape(side * set_rows, tracks).astype(BF16)
    bin_grad = jnp.dot(turned_ref[...], gene_grad, preferred_element_type=F32)
    logit_grad = (bin_grad * slope_ref[...]).astype(BF16)

    core = at_ref[1]
    for x in range(xs):
        for ref, upper in ((ours_ref, 2 * x + core), (other_ref, 2 * x + 1 - core)):
            lhs = jnp.concatenate([ref[x, w] for w in range(windows)], axis=1)
            grad = jnp.dot(lhs, logit_grad, preferred_element_type=F32)
            for i in range(side):
                place = upper * at_ref[3] + i * at_ref[4]
                sent_ref[place] = grad[i * padded : (i + 1) * padded].astype(BF16)


def fold_kernel(got_ref, sent_ref):
    for i in range(sent_ref.shape[0]):
        total = got_ref[0, i].astype(F32)
        for j in range(1, got_ref.shape[0]):
            total += got_ref[j, i].astype(F32)
        sent_ref[i] = (total * jnp.abs(total)).astype(BF16)


def per_device(embeddings, head, exon_starts, exon_lengths, gene_owner, gene_targets):
    places = lax.axis_size(SEQ)
    place = lax.axis_index(SEQ)
    core = lax.axis_index("c")
    side = lax.axis_size("y")
    windows, bin_dev, channels_dev = embeddings.shape
    channels, tracks = head.shape
    genes = gene_owner.shape[1]
    capacity = gene_targets.shape[1]
    held = genes // places
    per_place = windows * held
    rows = places * per_place
    xs, cores = lax.axis_size("x"), lax.axis_size("c")
    parts = xs * cores
    block = channels // places
    padded = -(-block // 16) * 16
    blocks_dev = channels_dev // block
    depth = blocks_dev * padded
    set_rows = rows // side
    side_rows = 2 * windows
    ahead, after = mixed_groups((side, places // side, xs, cores))

    packed = pl.pallas_call(
        lambda *refs: pack_kernel(block, padded, *refs),
        out_shape=jax.ShapeDtypeStruct((xs, windows, depth, bin_dev), BF16),
        in_specs=[VMEM],
        out_specs=VMEM,
        compiler_params=SMALL,
        name="pack",
    )(embeddings.transpose(0, 2, 1))
    ours = exchange(packed, "x")

    padded_head = jnp.pad(head.reshape(places, block, tracks), ((0, 0), (0, padded - block), (0, 0)))
    padded_head = padded_head.reshape(parts, depth, tracks)

    first = core == 0
    axis = jnp.where(first, lax.axis_index("y"), lax.axis_index("z"))
    at = jnp.stack([place, core, axis, jnp.where(first, side, 1), jnp.where(first, 1, side)]).astype(jnp.int32)

    plan = pl.pallas_call(
        lambda *refs: plan_kernel(places, *refs),
        out_shape=[
            jax.ShapeDtypeStruct((rows, windows * bin_dev), BF16),
            jax.ShapeDtypeStruct((windows * bin_dev, rows), BF16),
            jax.ShapeDtypeStruct((side, side_rows, tracks), BF16),
            jax.ShapeDtypeStruct((set_rows, places * windows), BF16),
            jax.ShapeDtypeStruct((windows * capacity, rows), F32),
        ],
        in_specs=[SMEM] + [VMEM] * 4,
        out_specs=[VMEM] * 5,
        compiler_params=SMALL,
        name="plan",
    )(at, gene_owner, exon_starts.transpose(0, 2, 1), exon_lengths.transpose(0, 2, 1), gene_targets)
    ours, padded_head, plan = lax.optimization_barrier((ours, padded_head, tuple(plan)))
    cover, turned, target_rows, pick, mine = plan
    other = lax.ppermute(ours, "c", [(0, 1), (1, 0)])

    sent, slope = pl.pallas_call(
        forward_kernel,
        out_shape=[
            jax.ShapeDtypeStruct((side, set_rows + side_rows, tracks), BF16),
            jax.ShapeDtypeStruct((windows * bin_dev, tracks), F32),
        ],
        in_specs=[SMEM] + [VMEM] * 5,
        out_specs=[VMEM] * 2,
        scratch_shapes=[pltpu.VMEM((windows * bin_dev, tracks), BF16)],
        compiler_params=SMALL,
        name="forward",
    )(at, ours, other, padded_head, cover, target_rows)

    sent = pl.pallas_call(
        lambda *refs: second_kernel(windows, *refs),
        out_shape=jax.ShapeDtypeStruct((side, set_rows + side * windows, tracks), BF16),
        in_specs=[VMEM],
        out_specs=VMEM,
        compiler_params=SMALL,
        name="second",
    )(exchange(sent, EVERY, ahead))
    sent = pl.pallas_call(
        lambda *refs: third_kernel(windows, *refs),
        out_shape=jax.ShapeDtypeStruct((side, set_rows + 6 * windows, tracks), BF16),
        in_specs=[VMEM, VMEM],
        out_specs=VMEM,
        compiler_params=SMALL,
        name="third",
    )(exchange(sent, EVERY, after), pick)
    got = exchange(sent, EVERY, ahead)

    sent, loss = pl.pallas_call(
        lambda *refs: backward_kernel(genes, *refs),
        out_shape=[
            jax.ShapeDtypeStruct((places, padded, tracks), BF16),
            jax.ShapeDtypeStruct((windows, tracks), F32),
        ],
        in_specs=[SMEM] + [VMEM] * 5,
        out_specs=[VMEM] * 2,
        compiler_params=SMALL,
        name="backward",
    )(at, got, turned, slope, ours, other)

    summed = exchange(sent.reshape(side, side * padded, tracks), EVERY, ahead)
    summed = pl.pallas_call(
        fold_kernel,
        out_shape=jax.ShapeDtypeStruct((side, padded, tracks), BF16),
        in_specs=[VMEM],
        out_specs=VMEM,
        compiler_params=SMALL,
        name="fold",
    )(summed.reshape(side, side, padded, tracks))
    summed, got, mine, loss, gene_targets = lax.optimization_barrier((summed, got, mine, loss, gene_targets))
    grads = exchange(summed, EVERY, after)[:, :block].astype(F32)
    root = jnp.sqrt(jnp.abs(grads))
    grad_head = jnp.sum(jnp.where(grads < 0, -root, root), axis=0)

    ratios = got[:, :set_rows].reshape(rows, tracks)
    back = jnp.dot(mine.astype(BF16), ratios, preferred_element_type=F32)
    valid = jnp.sum(mine, axis=1, keepdims=True) > 0
    targets_here = gene_targets.reshape(windows * capacity, tracks)
    gene_here = jnp.where(valid, targets_here / rooted(jnp.where(valid, back, 1.0)), 0.0)
    return (gene_here.reshape(gene_targets.shape), loss, grad_head)


def solution(mesh):
    shape = (8, 8, 4, 2)
    fine = Mesh(mesh.devices.reshape(shape), EVERY)
    return jax.shard_map(
        per_device,
        mesh=fine,
        in_specs=(P(None, SEQ, ("x", "c")), P(None, ("x", "c")), P(), P(), P(), P(None, SEQ, ("x", "c"))),
        out_specs=(P(None, SEQ, ("x", "c")), P(None, ("x", "c")), P(SEQ, ("x", "c"))),
        check_vma=False,
    )
```

```python
import jax
import jax.numpy as jnp
import numpy as np
from jax import lax
from jax.experimental import pallas as pl
from jax.experimental.pallas import tpu as pltpu
from jax.sharding import Mesh, PartitionSpec as P

SEQ = ("y", "z")
EVERY = ("y", "z", "x", "c")
F32 = jnp.float32
BF16 = jnp.bfloat16
MIDDLE = 28.28
VMEM = pl.BlockSpec(memory_space=pltpu.VMEM)
SMEM = pl.BlockSpec(memory_space=pltpu.SMEM)
HBM = pl.BlockSpec(memory_space=pltpu.HBM)
SMALL = pltpu.CompilerParams(vmem_limit_bytes=16 * 1024 * 1024)


def exchange(blocks, axes, groups=None):
    return lax.all_to_all(blocks, axes, split_axis=0, concat_axis=0, axis_index_groups=groups, tiled=True)


def mixed_groups(shape):
    ids = np.arange(int(np.prod(shape))).reshape(shape)
    ahead, after = [], []
    for x in range(shape[2]):
        for k in range(shape[0]):
            ahead += [ids[:, k, x, 0].tolist(), ids[k, :, x, 1].tolist()]
            after += [ids[k, :, x, 0].tolist(), ids[:, k, x, 1].tolist()]
    return ahead, after


def spread(counts, middle=MIDDLE):
    scaled = counts * (1.0 / middle)
    for _ in range(4):
        scaled = scaled * scaled
    return scaled


def unspread(coded, middle=MIDDLE):
    for _ in range(4):
        coded = jnp.sqrt(coded)
    return coded * middle


def squared(ratio):
    small = ratio < 2.0**63
    scaled = jnp.where(small, ratio, ratio * 2.0**-96)
    return jnp.where(small, scaled * scaled, -(scaled * scaled))


def rooted(coded):
    root = jnp.sqrt(jnp.abs(coded))
    return jnp.where(coded < 0, root * 2.0**96, root)


def split(values):
    high = values.astype(BF16).astype(F32)
    return high, values - high


def packed_sum(partial):
    tiny = partial < 2.0**-40
    scaled = jnp.where(tiny, partial * 2.0**80, partial)
    return jnp.where(tiny, -(scaled * scaled), scaled * scaled)


def unpacked_sum(coded):
    root = jnp.sqrt(jnp.abs(coded))
    return jnp.where(coded < 0, root * 2.0**-80, root)


def pack_kernel(block, padded, local_ref, packed_ref, raw_ref, rows_ref, arrived, left):
    copies, windows, depth, bins = packed_ref.shape
    reads = [pltpu.make_async_copy(local_ref.at[w], raw_ref.at[w], arrived.at[w]) for w in range(windows)]
    for read in reads:
        read.start()
    writes = []
    for w in range(windows):
        reads[w].wait()
        rows = raw_ref[w].astype(F32)
        gap = jnp.zeros((padded - block, bins), F32)
        pieces = []
        for i in range(depth // padded):
            pieces += [rows[i * block : (i + 1) * block], gap]
        rows_ref[w] = jnp.concatenate(pieces, axis=0).astype(BF16)
        for i in range(copies):
            write = pltpu.make_async_copy(rows_ref.at[w], packed_ref.at[i, w], left.at[w, i])
            write.start()
            writes.append(write)
    for write in writes:
        write.wait()


def ordering(at_ref, owner_ref, w, places, side, set_rows):
    windows, genes = owner_ref.shape
    square = (genes, genes)
    owner = owner_ref[w : w + 1, :]
    high = owner // side
    key = jnp.where(at_ref[1] == 0, (owner - high * side) * side + high, owner)
    other = jnp.broadcast_to(key.astype(F32), square)
    own = other.T
    earlier = lax.broadcasted_iota(jnp.int32, square, 1) < lax.broadcasted_iota(jnp.int32, square, 0)
    ahead = jnp.where((other == own) & earlier, 1.0, 0.0)
    rank = jnp.sum(ahead, axis=1, keepdims=True)
    at = jnp.sum(jnp.where(other < own, 1.0, ahead), axis=1, keepdims=True).astype(jnp.int32)
    turn = at // places
    place_of = at - turn * places
    high = place_of // side
    part = place_of - high * side
    row = w * (set_rows // windows) + high * (genes // places) + turn
    return own[:, :1].astype(jnp.int32), rank, at, part, row


def cover_kernel(places, side, at_ref, owner_ref, starts_ref, lengths_ref, cover_ref, turned_ref):
    windows, genes = owner_ref.shape
    exons = starts_ref.shape[1]
    rows, width = cover_ref.shape
    bins = width // windows
    set_rows = rows // side
    position = lax.broadcasted_iota(jnp.int32, (bins, genes), 0) + at_ref[0] * bins
    lane = lax.broadcasted_iota(jnp.int32, (genes, rows), 1)
    for w in range(windows):
        _, _, _, part, row = ordering(at_ref, owner_ref, w, places, side, set_rows)
        spot = jnp.where(part * set_rows + row == lane, 1.0, 0.0).astype(BF16)
        base = jnp.zeros((bins, genes), F32)
        for e in range(exons):
            past = position - starts_ref[w, e : e + 1, :]
            base += jnp.where((past >= 0) & (past < lengths_ref[w, e : e + 1, :]), 1.0, 0.0)
        turned = jnp.dot(base.astype(BF16), spot, preferred_element_type=F32)
        turned_ref[w * bins : (w + 1) * bins, :] = turned.astype(BF16)
        cover_ref[:, w * bins : (w + 1) * bins] = turned.T.astype(BF16)


def plan_kernel(places, at_ref, owner_ref, counts_ref, target_ref, keep_ref, pick_ref, mine_ref):
    windows, genes = owner_ref.shape
    capacity, tracks = counts_ref.shape[1:]
    side, sent_rows = target_ref.shape[:2]
    rows = mine_ref.shape[1]
    set_rows, sources = pick_ref.shape
    axis, column = at_ref[2], at_ref[5]
    lane = lax.broadcasted_iota(jnp.int32, (genes, rows), 1)
    targets = jnp.zeros((side * sent_rows, tracks), F32)
    keep = jnp.zeros(keep_ref.shape, F32)
    pick = jnp.zeros((set_rows, sources), F32)
    across = (((0,), (0,)), ((), ()))
    for w in range(windows):
        key, rank, at, part, row = ordering(at_ref, owner_ref, w, places, side, set_rows)
        spot = jnp.where(part * set_rows + row == lane, 1.0, 0.0)
        second = key // side
        first = key - second * side
        spare = w * capacity + (at // side) % capacity
        ours = part == axis
        here = jnp.where(ours & (row == lane[:, :set_rows]), 1.0, 0.0).astype(BF16)
        source = second * (sources // side) + spare
        origin = jnp.where(source == lane[:, :sources], 1.0, 0.0).astype(BF16)
        pick += lax.dot_general(here, origin, across, preferred_element_type=F32)
        room = lane[:, : keep_ref.shape[0]]
        here = jnp.where(ours & (second == column) & (spare == room), 1.0, 0.0).astype(BF16)
        origin = jnp.where(first * sent_rows + w == lane[:, : side * sent_rows], 1.0, 0.0).astype(BF16)
        keep += lax.dot_general(here, origin, across, preferred_element_type=F32)

        owned = (first == axis) & (second == column)
        coded = jnp.zeros((genes, tracks), F32)
        for k in range(capacity):
            slot = owned & (rank == k)
            filled = jnp.sum(jnp.where(slot, 1.0, 0.0), axis=0, keepdims=True) > 0
            count = counts_ref[w, k : k + 1, :]
            count = spread(jnp.where(jnp.broadcast_to(filled, count.shape), count, 1.0))
            coded += jnp.where(jnp.broadcast_to(slot, coded.shape), jnp.broadcast_to(count, coded.shape), 0.0)
            mark = jnp.where(jnp.broadcast_to(slot, lane.shape), spot, 0.0)
            mine_ref[w * capacity + k : w * capacity + k + 1, :] = jnp.sum(mark, axis=0, keepdims=True)
        goes = jnp.where(part * sent_rows + w == lane[:, : side * sent_rows], 1.0, 0.0).astype(BF16)
        targets += lax.dot_general(goes, coded.astype(BF16), across, preferred_element_type=F32)
    target_ref[...] = targets.reshape(side, sent_rows, tracks).astype(BF16)
    keep_ref[...] = keep.astype(BF16)
    pick_ref[...] = pick.astype(BF16)


def forward_kernel(
    at_ref, ours_ref, theirs_ref, head_ref, cover_ref, target_ref, sent_ref, slope_ref, pred_ref, other_ref, arrived
):
    xs, windows, _, bins = ours_ref.shape
    core = at_ref[1]
    side, sent_rows, tracks = sent_ref.shape
    set_rows = sent_rows - target_ref.shape[1]
    copy = pltpu.make_async_copy(theirs_ref, other_ref, arrived)
    copy.start()

    def product(ref, w, core):
        logits = jnp.zeros((bins, tracks), F32)
        for x in range(xs):
            logits += lax.dot_general(
                ref[x, w], head_ref[2 * x + core], (((0,), (0,)), ((), ())), preferred_element_type=F32
            )
        return logits

    for w in range(windows):
        slope_ref[w * bins : (w + 1) * bins, :] = product(ours_ref, w, core)
    copy.wait()
    for w in range(windows):
        logits = slope_ref[w * bins : (w + 1) * bins, :] + product(other_ref, w, 1 - core)
        low = jnp.exp(-jnp.abs(logits))
        pred_ref[w * bins : (w + 1) * bins, :] = (jnp.maximum(logits, 0.0) + jnp.log1p(low)).astype(BF16)
        slope_ref[w * bins : (w + 1) * bins, :] = jnp.where(logits >= 0, 1.0, low) / (1.0 + low)
    partial = jnp.dot(cover_ref[...], pred_ref[...], preferred_element_type=F32)
    sent_ref[:, :set_rows, :] = packed_sum(partial).reshape(side, set_rows, tracks).astype(BF16)
    sent_ref[:, set_rows:, :] = target_ref[...]


def second_kernel(windows, got_ref, keep_ref, sent_ref):
    side, got_rows, tracks = got_ref.shape
    set_rows = got_rows - 2 * windows
    total = unpacked_sum(got_ref[0, :set_rows, :].astype(F32))
    for i in range(1, side):
        total += unpacked_sum(got_ref[i, :set_rows, :].astype(F32))
    rows = got_ref[:, set_rows:, :].astype(F32).reshape(keep_ref.shape[1], tracks).astype(BF16)
    kept = jnp.dot(keep_ref[...], rows, preferred_element_type=F32)
    block = jnp.concatenate([packed_sum(total), kept], axis=0).astype(BF16)
    for i in range(side):
        sent_ref[i] = block


def third_kernel(windows, got_ref, pick_ref, sent_ref):
    side, got_rows, tracks = got_ref.shape
    set_rows, sources = pick_ref.shape
    gene_pred = unpacked_sum(got_ref[0, :set_rows, :].astype(F32))
    for i in range(1, side):
        gene_pred += unpacked_sum(got_ref[i, :set_rows, :].astype(F32))
    rows = got_ref[:, set_rows:, :].astype(F32).reshape(sources, tracks).astype(BF16)
    gene_target = unspread(jnp.dot(pick_ref[...], rows, preferred_element_type=F32))
    total, target_sum, fit = [
        jnp.sum(values.reshape(windows, set_rows // windows, tracks), axis=1)
        for values in (gene_pred, gene_target, gene_target * jnp.log(gene_pred))
    ]
    target_sum = spread(target_sum, MIDDLE * (set_rows // windows))
    pieces = [squared(gene_target / gene_pred), *split(total), target_sum, fit]
    block = jnp.concatenate(pieces, axis=0).astype(BF16)
    for i in range(side):
        sent_ref[i] = block


def backward_kernel(
    genes, at_ref, got_ref, turned_ref, slope_ref, ours_ref, other_ref, mine_ref, counts_ref, sent_ref, loss_ref, gene_ref
):
    side, got_rows, tracks = got_ref.shape
    xs, windows, depth, bins = ours_ref.shape
    set_rows = got_rows - 4 * windows
    window_rows = set_rows // windows
    padded = sent_ref.shape[1]
    sums = got_ref[:, set_rows:, :].astype(F32)
    high, low, target_sum, fit = [sums[:, i * windows : (i + 1) * windows, :] for i in range(4)]
    total = jnp.sum(high, axis=0) + jnp.sum(low, axis=0)
    target_sum = jnp.sum(unspread(target_sum, MIDDLE * window_rows), axis=0)
    fit = jnp.sum(fit, axis=0)
    log_total = jnp.log(total)
    loss_ref[...] = (-fit + target_sum * log_total + 0.2 * (total - target_sum * log_total)) / target_sum
    scale = genes / target_sum
    level = scale * (0.2 + 0.8 * target_sum / total)
    grads = []
    for w in range(windows):
        ratio = rooted(got_ref[:, w * window_rows : (w + 1) * window_rows, :].astype(F32))
        grads.append(level[w : w + 1][None] - scale[w : w + 1][None] * ratio)
    gene_grad = jnp.concatenate(grads, axis=1).reshape(side * set_rows, tracks).astype(BF16)
    bin_grad = jnp.dot(turned_ref[...], gene_grad, preferred_element_type=F32)
    logit_grad = (bin_grad * slope_ref[...]).astype(BF16)

    capacity = counts_ref.shape[1]
    ratios = got_ref[:, :set_rows, :].reshape(side * set_rows, tracks)
    back = jnp.dot(mine_ref[...].astype(BF16), ratios, preferred_element_type=F32)
    filled = jnp.sum(mine_ref[...], axis=1, keepdims=True) > 0
    back = rooted(jnp.where(jnp.broadcast_to(filled, back.shape), back, 1.0))
    back = jnp.where(jnp.broadcast_to(filled, back.shape), 1.0 / back, 0.0)
    for w in range(windows):
        here = back[w * capacity : (w + 1) * capacity]
        gene_ref[w] = jnp.where(here > 0, counts_ref[w] * here, 0.0)

    core = at_ref[1]
    for x in range(xs):
        for ref, upper in ((ours_ref, 2 * x + core), (other_ref, 2 * x + 1 - core)):
            lhs = jnp.concatenate([ref[x, w] for w in range(windows)], axis=1)
            grad = jnp.dot(lhs, logit_grad, preferred_element_type=F32)
            for i in range(side):
                place = upper * at_ref[3] + i * at_ref[4]
                sent_ref[place] = grad[i * padded : (i + 1) * padded].astype(BF16)


def fold_kernel(got_ref, sent_ref):
    for i in range(sent_ref.shape[0]):
        total = got_ref[0, i].astype(F32)
        for j in range(1, got_ref.shape[0]):
            total += got_ref[j, i].astype(F32)
        sent_ref[i] = (total * jnp.abs(total)).astype(BF16)


def per_device(embeddings, head, exon_starts, exon_lengths, gene_owner, gene_targets):
    places = lax.axis_size(SEQ)
    place = lax.axis_index(SEQ)
    core = lax.axis_index("c")
    side = lax.axis_size("y")
    windows, bin_dev, channels_dev = embeddings.shape
    channels, tracks = head.shape
    genes = gene_owner.shape[1]
    capacity = gene_targets.shape[1]
    held = genes // places
    per_place = windows * held
    rows = places * per_place
    xs, cores = lax.axis_size("x"), lax.axis_size("c")
    parts = xs * cores
    block = channels // places
    padded = -(-block // 16) * 16
    blocks_dev = channels_dev // block
    depth = blocks_dev * padded
    set_rows = rows // side
    side_rows = 2 * windows
    ahead, after = mixed_groups((side, places // side, xs, cores))

    packed = pl.pallas_call(
        lambda *refs: pack_kernel(block, padded, *refs),
        out_shape=jax.ShapeDtypeStruct((xs, windows, depth, bin_dev), BF16),
        in_specs=[HBM],
        out_specs=HBM,
        scratch_shapes=[
            pltpu.VMEM((windows, channels_dev, bin_dev), BF16),
            pltpu.VMEM((windows, depth, bin_dev), BF16),
            pltpu.SemaphoreType.DMA((windows,)),
            pltpu.SemaphoreType.DMA((windows, xs)),
        ],
        name="pack",
    )(embeddings.transpose(0, 2, 1))
    ours = exchange(packed, "x")

    padded_head = jnp.pad(head.reshape(places, block, tracks), ((0, 0), (0, padded - block), (0, 0)))
    padded_head = padded_head.reshape(parts, depth, tracks)

    first = core == 0
    y, z = lax.axis_index("y"), lax.axis_index("z")
    axis, column = jnp.where(first, y, z), jnp.where(first, z, y)
    at = jnp.stack([place, core, axis, jnp.where(first, side, 1), jnp.where(first, 1, side), column])
    at = at.astype(jnp.int32)

    plan = pl.pallas_call(
        lambda *refs: plan_kernel(places, *refs),
        out_shape=[
            jax.ShapeDtypeStruct((side, side_rows, tracks), BF16),
            jax.ShapeDtypeStruct((windows * capacity, side * side_rows), BF16),
            jax.ShapeDtypeStruct((set_rows, side * windows * capacity), BF16),
            jax.ShapeDtypeStruct((windows * capacity, rows), F32),
        ],
        in_specs=[SMEM, VMEM, VMEM],
        out_specs=[VMEM] * 4,
        compiler_params=SMALL,
        name="plan",
    )(at, gene_owner, gene_targets)
    ours, padded_head, plan, starts, lengths = lax.optimization_barrier(
        (ours, padded_head, tuple(plan), exon_starts.transpose(0, 2, 1), exon_lengths.transpose(0, 2, 1))
    )
    target_rows, keep, pick, mine = plan
    other = lax.ppermute(ours, "c", [(0, 1), (1, 0)])
    cover, turned = pl.pallas_call(
        lambda *refs: cover_kernel(places, side, *refs),
        out_shape=[
            jax.ShapeDtypeStruct((rows, windows * bin_dev), BF16),
            jax.ShapeDtypeStruct((windows * bin_dev, rows), BF16),
        ],
        in_specs=[SMEM] + [VMEM] * 3,
        out_specs=[VMEM] * 2,
        compiler_params=SMALL,
        name="cover",
    )(at, gene_owner, starts, lengths)

    sent, slope = pl.pallas_call(
        forward_kernel,
        out_shape=[
            jax.ShapeDtypeStruct((side, set_rows + side_rows, tracks), BF16),
            jax.ShapeDtypeStruct((windows * bin_dev, tracks), F32),
        ],
        in_specs=[SMEM, VMEM, HBM, VMEM, VMEM, VMEM],
        out_specs=[VMEM] * 2,
        scratch_shapes=[
            pltpu.VMEM((windows * bin_dev, tracks), BF16),
            pltpu.VMEM((xs, windows, depth, bin_dev), BF16),
            pltpu.SemaphoreType.DMA,
        ],
        compiler_params=SMALL,
        name="forward",
    )(at, ours, other, padded_head, cover, target_rows)

    sent = pl.pallas_call(
        lambda *refs: second_kernel(windows, *refs),
        out_shape=jax.ShapeDtypeStruct((side, set_rows + windows * capacity, tracks), BF16),
        in_specs=[VMEM, VMEM],
        out_specs=VMEM,
        compiler_params=SMALL,
        name="second",
    )(exchange(sent, EVERY, ahead), keep)
    sent = pl.pallas_call(
        lambda *refs: third_kernel(windows, *refs),
        out_shape=jax.ShapeDtypeStruct((side, set_rows + 4 * windows, tracks), BF16),
        in_specs=[VMEM, VMEM],
        out_specs=VMEM,
        compiler_params=SMALL,
        name="third",
    )(exchange(sent, EVERY, after), pick)
    got = exchange(sent, EVERY, ahead)

    sent, loss, gene_here = pl.pallas_call(
        lambda *refs: backward_kernel(genes, *refs),
        out_shape=[
            jax.ShapeDtypeStruct((places, padded, tracks), BF16),
            jax.ShapeDtypeStruct((windows, tracks), F32),
            jax.ShapeDtypeStruct(gene_targets.shape, F32),
        ],
        in_specs=[SMEM] + [VMEM] * 7,
        out_specs=[VMEM] * 3,
        compiler_params=SMALL,
        name="backward",
    )(at, got, turned, slope, ours, other, mine, gene_targets)

    summed = exchange(sent.reshape(side, side * padded, tracks), EVERY, ahead)
    summed = pl.pallas_call(
        fold_kernel,
        out_shape=jax.ShapeDtypeStruct((side, padded, tracks), BF16),
        in_specs=[VMEM],
        out_specs=VMEM,
        compiler_params=SMALL,
        name="fold",
    )(summed.reshape(side, side, padded, tracks))
    grads = exchange(summed, EVERY, after)[:, :block].astype(F32)
    root = jnp.sqrt(jnp.abs(grads))
    grad_head = jnp.sum(jnp.where(grads < 0, -root, root), axis=0)

    return (gene_here, loss, grad_head)


def solution(mesh):
    shape = (8, 8, 4, 2)
    fine = Mesh(mesh.devices.reshape(shape), EVERY)
    return jax.shard_map(
        per_device,
        mesh=fine,
        in_specs=(P(None, SEQ, ("x", "c")), P(None, ("x", "c")), P(), P(), P(), P(None, SEQ, ("x", "c"))),
        out_specs=(P(None, SEQ, ("x", "c")), P(None, ("x", "c")), P(SEQ, ("x", "c"))),
        check_vma=False,
    )
```

```python
import jax
import jax.numpy as jnp
import numpy as np
from jax import lax
from jax.experimental import pallas as pl
from jax.experimental.pallas import tpu as pltpu
from jax.sharding import Mesh, PartitionSpec as P

SEQ = ("y", "z")
EVERY = ("y", "z", "x", "c")
F32 = jnp.float32
BF16 = jnp.bfloat16
MIDDLE = 28.28
VMEM = pl.BlockSpec(memory_space=pltpu.VMEM)
SMEM = pl.BlockSpec(memory_space=pltpu.SMEM)
HBM = pl.BlockSpec(memory_space=pltpu.HBM)
SMALL = pltpu.CompilerParams(vmem_limit_bytes=16 * 1024 * 1024)


def exchange(blocks, axes, groups=None):
    return lax.all_to_all(blocks, axes, split_axis=0, concat_axis=0, axis_index_groups=groups, tiled=True)


def mixed_groups(shape):
    ids = np.arange(int(np.prod(shape))).reshape(shape)
    ahead, after = [], []
    for x in range(shape[2]):
        for k in range(shape[0]):
            ahead += [ids[:, k, x, 0].tolist(), ids[k, :, x, 1].tolist()]
            after += [ids[k, :, x, 0].tolist(), ids[:, k, x, 1].tolist()]
    return ahead, after


def spread(counts, middle=MIDDLE):
    scaled = counts * (1.0 / middle)
    for _ in range(4):
        scaled = scaled * scaled
    return scaled


def unspread(coded, middle=MIDDLE):
    for _ in range(4):
        coded = jnp.sqrt(coded)
    return coded * middle


def squared(ratio):
    small = ratio < 2.0**63
    scaled = jnp.where(small, ratio, ratio * 2.0**-96)
    return jnp.where(small, scaled * scaled, -(scaled * scaled))


def rooted(coded):
    root = jnp.sqrt(jnp.abs(coded))
    return jnp.where(coded < 0, root * 2.0**96, root)


def split(values):
    high = values.astype(BF16).astype(F32)
    return high, values - high


def packed_sum(partial):
    tiny = partial < 2.0**-40
    scaled = jnp.where(tiny, partial * 2.0**80, partial)
    return jnp.where(tiny, -(scaled * scaled), scaled * scaled)


def unpacked_sum(coded):
    root = jnp.sqrt(jnp.abs(coded))
    return jnp.where(coded < 0, root * 2.0**-80, root)


def pack_kernel(block, padded, local_ref, packed_ref, raw_ref, rows_ref, arrived, left):
    copies, windows, depth, bins = packed_ref.shape
    reads = [pltpu.make_async_copy(local_ref.at[w], raw_ref.at[w], arrived.at[w]) for w in range(windows)]
    for read in reads:
        read.start()
    writes = []
    for w in range(windows):
        reads[w].wait()
        rows = raw_ref[w].astype(F32)
        gap = jnp.zeros((padded - block, bins), F32)
        pieces = []
        for i in range(depth // padded):
            pieces += [rows[i * block : (i + 1) * block], gap]
        rows_ref[w] = jnp.concatenate(pieces, axis=0).astype(BF16)
        for i in range(copies):
            write = pltpu.make_async_copy(rows_ref.at[w], packed_ref.at[i, w], left.at[w, i])
            write.start()
            writes.append(write)
    for write in writes:
        write.wait()


def ordering(at_ref, owner_ref, w, places, side, set_rows):
    windows, genes = owner_ref.shape
    square = (genes, genes)
    owner = owner_ref[w : w + 1, :]
    high = owner // side
    key = jnp.where(at_ref[1] == 0, (owner - high * side) * side + high, owner)
    other = jnp.broadcast_to(key.astype(F32), square)
    own = other.T
    earlier = lax.broadcasted_iota(jnp.int32, square, 1) < lax.broadcasted_iota(jnp.int32, square, 0)
    ahead = jnp.where((other == own) & earlier, 1.0, 0.0)
    rank = jnp.sum(ahead, axis=1, keepdims=True)
    at = jnp.sum(jnp.where(other < own, 1.0, ahead), axis=1, keepdims=True).astype(jnp.int32)
    turn = at // places
    place_of = at - turn * places
    high = place_of // side
    part = place_of - high * side
    row = w * (set_rows // windows) + high * (genes // places) + turn
    return own[:, :1].astype(jnp.int32), rank, at, part, row


def cover_kernel(at_ref, spots_ref, starts_ref, lengths_ref, cover_ref, turned_ref):
    windows, exons, genes = starts_ref.shape
    rows, width = cover_ref.shape
    bins = width // windows
    position = lax.broadcasted_iota(jnp.int32, (bins, genes), 0) + at_ref[0] * bins
    lane = lax.broadcasted_iota(jnp.int32, (genes, rows), 1)
    for w in range(windows):
        spot = jnp.where(spots_ref[:, w : w + 1] == lane, 1.0, 0.0).astype(BF16)
        base = jnp.zeros((bins, genes), F32)
        for e in range(exons):
            past = position - starts_ref[w, e : e + 1, :]
            base += jnp.where((past >= 0) & (past < lengths_ref[w, e : e + 1, :]), 1.0, 0.0)
        turned = jnp.dot(base.astype(BF16), spot, preferred_element_type=F32)
        turned_ref[w * bins : (w + 1) * bins, :] = turned.astype(BF16)
        cover_ref[:, w * bins : (w + 1) * bins] = turned.T.astype(BF16)


def plan_kernel(places, at_ref, owner_ref, counts_ref, target_ref, keep_ref, pick_ref, mine_ref, spots_ref):
    windows, genes = owner_ref.shape
    capacity, tracks = counts_ref.shape[1:]
    side, sent_rows = target_ref.shape[:2]
    rows = mine_ref.shape[1]
    set_rows, sources = pick_ref.shape
    axis, column = at_ref[2], at_ref[5]
    lane = lax.broadcasted_iota(jnp.int32, (genes, rows), 1)
    targets = jnp.zeros((side * sent_rows, tracks), F32)
    keep = jnp.zeros(keep_ref.shape, F32)
    pick = jnp.zeros((set_rows, sources), F32)
    across = (((0,), (0,)), ((), ()))
    for w in range(windows):
        key, rank, at, part, row = ordering(at_ref, owner_ref, w, places, side, set_rows)
        spot = jnp.where(part * set_rows + row == lane, 1.0, 0.0)
        spots_ref[:, w : w + 1] = part * set_rows + row
        second = key // side
        first = key - second * side
        spare = w * capacity + (at // side) % capacity
        ours = part == axis
        here = jnp.where(ours & (row == lane[:, :set_rows]), 1.0, 0.0).astype(BF16)
        source = second * (sources // side) + spare
        origin = jnp.where(source == lane[:, :sources], 1.0, 0.0).astype(BF16)
        pick += lax.dot_general(here, origin, across, preferred_element_type=F32)
        room = lane[:, : keep_ref.shape[0]]
        here = jnp.where(ours & (second == column) & (spare == room), 1.0, 0.0).astype(BF16)
        origin = jnp.where(first * sent_rows + w == lane[:, : side * sent_rows], 1.0, 0.0).astype(BF16)
        keep += lax.dot_general(here, origin, across, preferred_element_type=F32)

        owned = (first == axis) & (second == column)
        coded = jnp.zeros((genes, tracks), F32)
        for k in range(capacity):
            slot = owned & (rank == k)
            filled = jnp.sum(jnp.where(slot, 1.0, 0.0), axis=0, keepdims=True) > 0
            count = counts_ref[w, k : k + 1, :]
            count = spread(jnp.where(jnp.broadcast_to(filled, count.shape), count, 1.0))
            coded += jnp.where(jnp.broadcast_to(slot, coded.shape), jnp.broadcast_to(count, coded.shape), 0.0)
            mark = jnp.where(jnp.broadcast_to(slot, lane.shape), spot, 0.0)
            mine_ref[w * capacity + k : w * capacity + k + 1, :] = jnp.sum(mark, axis=0, keepdims=True)
        goes = jnp.where(part * sent_rows + w == lane[:, : side * sent_rows], 1.0, 0.0).astype(BF16)
        targets += lax.dot_general(goes, coded.astype(BF16), across, preferred_element_type=F32)
    target_ref[...] = targets.reshape(side, sent_rows, tracks).astype(BF16)
    keep_ref[...] = keep.astype(BF16)
    pick_ref[...] = pick.astype(BF16)


def half_product(core, ref, head_ref):
    xs, windows, _, bins = ref.shape
    columns = [jnp.concatenate([ref[x, w] for w in range(windows)], axis=1) for x in range(xs)]
    weights = [head_ref[2 * x + core] for x in range(xs)]
    return lax.dot_general(
        jnp.concatenate(columns, axis=0),
        jnp.concatenate(weights, axis=0),
        (((0,), (0,)), ((), ())),
        preferred_element_type=F32,
    )


def half_kernel(at_ref, ours_ref, head_ref, logits_ref):
    logits_ref[...] = half_product(at_ref[1], ours_ref, head_ref)


def forward_kernel(
    at_ref, half_ref, other_ref, head_ref, cover_ref, target_ref, sent_ref, slope_ref, pred_ref
):
    side, sent_rows, tracks = sent_ref.shape
    set_rows = sent_rows - target_ref.shape[1]
    logits = half_ref[...] + half_product(1 - at_ref[1], other_ref, head_ref)
    low = jnp.exp(-jnp.abs(logits))
    pred_ref[...] = (jnp.maximum(logits, 0.0) + jnp.log1p(low)).astype(BF16)
    slope_ref[...] = jnp.where(logits >= 0, 1.0, low) / (1.0 + low)
    partial = jnp.dot(cover_ref[...], pred_ref[...], preferred_element_type=F32)
    sent_ref[:, :set_rows, :] = packed_sum(partial).reshape(side, set_rows, tracks).astype(BF16)
    sent_ref[:, set_rows:, :] = target_ref[...]


def second_kernel(windows, got_ref, keep_ref, sent_ref):
    side, got_rows, tracks = got_ref.shape
    set_rows = got_rows - 2 * windows
    total = unpacked_sum(got_ref[0, :set_rows, :].astype(F32))
    for i in range(1, side):
        total += unpacked_sum(got_ref[i, :set_rows, :].astype(F32))
    rows = got_ref[:, set_rows:, :].astype(F32).reshape(keep_ref.shape[1], tracks).astype(BF16)
    kept = jnp.dot(keep_ref[...], rows, preferred_element_type=F32)
    block = jnp.concatenate([packed_sum(total), kept], axis=0).astype(BF16)
    for i in range(side):
        sent_ref[i] = block


def third_kernel(windows, got_ref, pick_ref, sent_ref):
    side, got_rows, tracks = got_ref.shape
    set_rows, sources = pick_ref.shape
    gene_pred = unpacked_sum(got_ref[0, :set_rows, :].astype(F32))
    for i in range(1, side):
        gene_pred += unpacked_sum(got_ref[i, :set_rows, :].astype(F32))
    rows = got_ref[:, set_rows:, :].astype(F32).reshape(sources, tracks).astype(BF16)
    gene_target = unspread(jnp.dot(pick_ref[...], rows, preferred_element_type=F32))
    total, target_sum, fit = [
        jnp.sum(values.reshape(windows, set_rows // windows, tracks), axis=1)
        for values in (gene_pred, gene_target, gene_target * jnp.log(gene_pred))
    ]
    target_sum = spread(target_sum, MIDDLE * (set_rows // windows))
    pieces = [squared(gene_target / gene_pred), *split(total), target_sum, fit]
    block = jnp.concatenate(pieces, axis=0).astype(BF16)
    for i in range(side):
        sent_ref[i] = block


def backward_kernel(
    genes, at_ref, got_ref, turned_ref, slope_ref, ours_ref, other_ref, mine_ref, counts_ref, sent_ref, loss_ref, gene_ref
):
    side, got_rows, tracks = got_ref.shape
    xs, windows, depth, bins = ours_ref.shape
    set_rows = got_rows - 4 * windows
    window_rows = set_rows // windows
    padded = sent_ref.shape[1]
    sums = got_ref[:, set_rows:, :].astype(F32)
    high, low, target_sum, fit = [sums[:, i * windows : (i + 1) * windows, :] for i in range(4)]
    total = jnp.sum(high, axis=0) + jnp.sum(low, axis=0)
    target_sum = jnp.sum(unspread(target_sum, MIDDLE * window_rows), axis=0)
    fit = jnp.sum(fit, axis=0)
    log_total = jnp.log(total)
    loss_ref[...] = (-fit + target_sum * log_total + 0.2 * (total - target_sum * log_total)) / target_sum
    scale = genes / target_sum
    level = scale * (0.2 + 0.8 * target_sum / total)
    grads = []
    for w in range(windows):
        ratio = rooted(got_ref[:, w * window_rows : (w + 1) * window_rows, :].astype(F32))
        grads.append(level[w : w + 1][None] - scale[w : w + 1][None] * ratio)
    gene_grad = jnp.concatenate(grads, axis=1).reshape(side * set_rows, tracks).astype(BF16)
    bin_grad = jnp.dot(turned_ref[...], gene_grad, preferred_element_type=F32)
    logit_grad = (bin_grad * slope_ref[...]).astype(BF16)

    capacity = counts_ref.shape[1]
    ratios = got_ref[:, :set_rows, :].reshape(side * set_rows, tracks)
    back = jnp.dot(mine_ref[...].astype(BF16), ratios, preferred_element_type=F32)
    filled = jnp.sum(mine_ref[...], axis=1, keepdims=True) > 0
    back = rooted(jnp.where(jnp.broadcast_to(filled, back.shape), back, 1.0))
    back = jnp.where(jnp.broadcast_to(filled, back.shape), 1.0 / back, 0.0)
    for w in range(windows):
        here = back[w * capacity : (w + 1) * capacity]
        gene_ref[w] = jnp.where(here > 0, counts_ref[w] * here, 0.0)

    core = at_ref[1]
    for ref, low in ((ours_ref, core), (other_ref, 1 - core)):
        lhs = [jnp.concatenate([ref[x, w] for w in range(windows)], axis=1) for x in range(xs)]
        grad = jnp.dot(jnp.concatenate(lhs, axis=0), logit_grad, preferred_element_type=F32).astype(BF16)
        for x in range(xs):
            for i in range(side):
                place = (2 * x + low) * at_ref[3] + i * at_ref[4]
                row = x * depth + i * padded
                sent_ref[place] = grad[row : row + padded]


def fold_kernel(got_ref, sent_ref):
    for i in range(sent_ref.shape[0]):
        total = got_ref[0, i].astype(F32)
        for j in range(1, got_ref.shape[0]):
            total += got_ref[j, i].astype(F32)
        sent_ref[i] = (total * jnp.abs(total)).astype(BF16)


def finish_kernel(got_ref, grad_ref):
    block = grad_ref.shape[0]
    total = jnp.zeros(got_ref.shape[1:], F32)
    for i in range(got_ref.shape[0]):
        grad = got_ref[i].astype(F32)
        root = jnp.sqrt(jnp.abs(grad))
        total += jnp.where(grad < 0, -root, root)
    grad_ref[...] = total[:block]


def per_device(embeddings, head, exon_starts, exon_lengths, gene_owner, gene_targets):
    places = lax.axis_size(SEQ)
    place = lax.axis_index(SEQ)
    core = lax.axis_index("c")
    side = lax.axis_size("y")
    windows, bin_dev, channels_dev = embeddings.shape
    channels, tracks = head.shape
    genes = gene_owner.shape[1]
    capacity = gene_targets.shape[1]
    held = genes // places
    per_place = windows * held
    rows = places * per_place
    xs, cores = lax.axis_size("x"), lax.axis_size("c")
    parts = xs * cores
    block = channels // places
    padded = -(-block // 16) * 16
    blocks_dev = channels_dev // block
    depth = blocks_dev * padded
    set_rows = rows // side
    side_rows = 2 * windows
    ahead, after = mixed_groups((side, places // side, xs, cores))

    packed = pl.pallas_call(
        lambda *refs: pack_kernel(block, padded, *refs),
        out_shape=jax.ShapeDtypeStruct((xs, windows, depth, bin_dev), BF16),
        in_specs=[HBM],
        out_specs=HBM,
        scratch_shapes=[
            pltpu.VMEM((windows, channels_dev, bin_dev), BF16),
            pltpu.VMEM((windows, depth, bin_dev), BF16),
            pltpu.SemaphoreType.DMA((windows,)),
            pltpu.SemaphoreType.DMA((windows, xs)),
        ],
        name="pack",
    )(embeddings.transpose(0, 2, 1))
    ours = exchange(packed, "x")

    padded_head = jnp.pad(head.reshape(places, block, tracks), ((0, 0), (0, padded - block), (0, 0)))
    padded_head = padded_head.reshape(parts, depth, tracks)

    first = core == 0
    y, z = lax.axis_index("y"), lax.axis_index("z")
    axis, column = jnp.where(first, y, z), jnp.where(first, z, y)
    at = jnp.stack([place, core, axis, jnp.where(first, side, 1), jnp.where(first, 1, side), column])
    at = at.astype(jnp.int32)

    plan = pl.pallas_call(
        lambda *refs: plan_kernel(places, *refs),
        out_shape=[
            jax.ShapeDtypeStruct((side, side_rows, tracks), BF16),
            jax.ShapeDtypeStruct((windows * capacity, side * side_rows), BF16),
            jax.ShapeDtypeStruct((set_rows, side * windows * capacity), BF16),
            jax.ShapeDtypeStruct((windows * capacity, rows), F32),
            jax.ShapeDtypeStruct((genes, 128), jnp.int32),
        ],
        in_specs=[SMEM, VMEM, VMEM],
        out_specs=[VMEM] * 5,
        compiler_params=SMALL,
        name="plan",
    )(at, gene_owner, gene_targets)
    ours, padded_head, plan, starts, lengths = lax.optimization_barrier(
        (ours, padded_head, tuple(plan), exon_starts.transpose(0, 2, 1), exon_lengths.transpose(0, 2, 1))
    )
    target_rows, keep, pick, mine, spots = plan
    other = lax.ppermute(ours, "c", [(0, 1), (1, 0)])
    cover, turned = pl.pallas_call(
        cover_kernel,
        out_shape=[
            jax.ShapeDtypeStruct((rows, windows * bin_dev), BF16),
            jax.ShapeDtypeStruct((windows * bin_dev, rows), BF16),
        ],
        in_specs=[SMEM] + [VMEM] * 3,
        out_specs=[VMEM] * 2,
        compiler_params=SMALL,
        name="cover",
    )(at, spots, starts, lengths)

    half = pl.pallas_call(
        half_kernel,
        out_shape=jax.ShapeDtypeStruct((windows * bin_dev, tracks), F32),
        in_specs=[SMEM, VMEM, VMEM],
        out_specs=VMEM,
        compiler_params=SMALL,
        name="half",
    )(at, ours, padded_head)

    sent, slope = pl.pallas_call(
        forward_kernel,
        out_shape=[
            jax.ShapeDtypeStruct((side, set_rows + side_rows, tracks), BF16),
            jax.ShapeDtypeStruct((windows * bin_dev, tracks), F32),
        ],
        in_specs=[SMEM] + [VMEM] * 5,
        out_specs=[VMEM] * 2,
        scratch_shapes=[pltpu.VMEM((windows * bin_dev, tracks), BF16)],
        compiler_params=SMALL,
        name="forward",
    )(at, half, other, padded_head, cover, target_rows)

    sent = pl.pallas_call(
        lambda *refs: second_kernel(windows, *refs),
        out_shape=jax.ShapeDtypeStruct((side, set_rows + windows * capacity, tracks), BF16),
        in_specs=[VMEM, VMEM],
        out_specs=VMEM,
        compiler_params=SMALL,
        name="second",
    )(exchange(sent, EVERY, ahead), keep)
    sent = pl.pallas_call(
        lambda *refs: third_kernel(windows, *refs),
        out_shape=jax.ShapeDtypeStruct((side, set_rows + 4 * windows, tracks), BF16),
        in_specs=[VMEM, VMEM],
        out_specs=VMEM,
        compiler_params=SMALL,
        name="third",
    )(exchange(sent, EVERY, after), pick)
    got = exchange(sent, EVERY, ahead)

    sent, loss, gene_here = pl.pallas_call(
        lambda *refs: backward_kernel(genes, *refs),
        out_shape=[
            jax.ShapeDtypeStruct((places, padded, tracks), BF16),
            jax.ShapeDtypeStruct((windows, tracks), F32),
            jax.ShapeDtypeStruct(gene_targets.shape, F32),
        ],
        in_specs=[SMEM] + [VMEM] * 7,
        out_specs=[VMEM] * 3,
        compiler_params=SMALL,
        name="backward",
    )(at, got, turned, slope, ours, other, mine, gene_targets)

    summed = exchange(sent.reshape(side, side * padded, tracks), EVERY, ahead)
    summed = pl.pallas_call(
        fold_kernel,
        out_shape=jax.ShapeDtypeStruct((side, padded, tracks), BF16),
        in_specs=[VMEM],
        out_specs=VMEM,
        compiler_params=SMALL,
        name="fold",
    )(summed.reshape(side, side, padded, tracks))
    grad_head = pl.pallas_call(
        finish_kernel,
        out_shape=jax.ShapeDtypeStruct((block, tracks), F32),
        in_specs=[VMEM],
        out_specs=VMEM,
        compiler_params=SMALL,
        name="finish",
    )(exchange(summed, EVERY, after))
    return (gene_here, loss, grad_head)


def solution(mesh):
    shape = (8, 8, 4, 2)
    fine = Mesh(mesh.devices.reshape(shape), EVERY)
    return jax.shard_map(
        per_device,
        mesh=fine,
        in_specs=(P(None, SEQ, ("x", "c")), P(None, ("x", "c")), P(), P(), P(), P(None, SEQ, ("x", "c"))),
        out_specs=(P(None, SEQ, ("x", "c")), P(None, ("x", "c")), P(SEQ, ("x", "c"))),
        check_vma=False,
    )
```

```python
import jax
import jax.numpy as jnp
import numpy as np
from jax import lax
from jax.experimental import pallas as pl
from jax.experimental.pallas import tpu as pltpu
from jax.sharding import Mesh, PartitionSpec as P

SEQ = ("y", "z")
EVERY = ("y", "z", "x", "c")
F32 = jnp.float32
BF16 = jnp.bfloat16
MIDDLE = 28.28
VMEM = pl.BlockSpec(memory_space=pltpu.VMEM)
SMEM = pl.BlockSpec(memory_space=pltpu.SMEM)
HBM = pl.BlockSpec(memory_space=pltpu.HBM)
SMALL = pltpu.CompilerParams(vmem_limit_bytes=16 * 1024 * 1024)


def exchange(blocks, axes, groups=None):
    return lax.all_to_all(blocks, axes, split_axis=0, concat_axis=0, axis_index_groups=groups, tiled=True)


def mixed_groups(shape):
    ids = np.arange(int(np.prod(shape))).reshape(shape)
    ahead, after = [], []
    for x in range(shape[2]):
        for k in range(shape[0]):
            ahead += [ids[:, k, x, 0].tolist(), ids[k, :, x, 1].tolist()]
            after += [ids[k, :, x, 0].tolist(), ids[:, k, x, 1].tolist()]
    return ahead, after


def spread(counts, middle=MIDDLE):
    scaled = counts * (1.0 / middle)
    for _ in range(4):
        scaled = scaled * scaled
    return scaled


def unspread(coded, middle=MIDDLE):
    for _ in range(4):
        coded = jnp.sqrt(coded)
    return coded * middle


def squared(ratio):
    small = ratio < 2.0**63
    scaled = jnp.where(small, ratio, ratio * 2.0**-96)
    return jnp.where(small, scaled * scaled, -(scaled * scaled))


def rooted(coded):
    root = jnp.sqrt(jnp.abs(coded))
    return jnp.where(coded < 0, root * 2.0**96, root)


def split(values):
    high = values.astype(BF16).astype(F32)
    return high, values - high


def packed_sum(partial):
    tiny = partial < 2.0**-40
    scaled = jnp.where(tiny, partial * 2.0**80, partial)
    return jnp.where(tiny, -(scaled * scaled), scaled * scaled)


def unpacked_sum(coded):
    root = jnp.sqrt(jnp.abs(coded))
    return jnp.where(coded < 0, root * 2.0**-80, root)


def pack_kernel(block, padded, local_ref, packed_ref, raw_ref, rows_ref, arrived, left):
    copies, windows, depth, bins = packed_ref.shape
    reads = [pltpu.make_async_copy(local_ref.at[w], raw_ref.at[w], arrived.at[w]) for w in range(windows)]
    for read in reads:
        read.start()
    writes = []
    for w in range(windows):
        reads[w].wait()
        rows = raw_ref[w].astype(F32)
        gap = jnp.zeros((padded - block, bins), F32)
        pieces = []
        for i in range(depth // padded):
            pieces += [rows[i * block : (i + 1) * block], gap]
        rows_ref[w] = jnp.concatenate(pieces, axis=0).astype(BF16)
        for i in range(copies):
            write = pltpu.make_async_copy(rows_ref.at[w], packed_ref.at[i, w], left.at[w, i])
            write.start()
            writes.append(write)
    for write in writes:
        write.wait()


def ordering(at_ref, owner_ref, w, places, side, set_rows):
    windows, genes = owner_ref.shape
    square = (genes, genes)
    owner = owner_ref[w : w + 1, :]
    high = owner // side
    key = jnp.where(at_ref[1] == 0, (owner - high * side) * side + high, owner)
    other = jnp.broadcast_to(key.astype(F32), square)
    own = other.T
    earlier = lax.broadcasted_iota(jnp.int32, square, 1) < lax.broadcasted_iota(jnp.int32, square, 0)
    ahead = jnp.where((other == own) & earlier, 1.0, 0.0)
    rank = jnp.sum(ahead, axis=1, keepdims=True)
    at = jnp.sum(jnp.where(other < own, 1.0, ahead), axis=1, keepdims=True).astype(jnp.int32)
    turn = at // places
    place_of = at - turn * places
    high = place_of // side
    part = place_of - high * side
    row = w * (set_rows // windows) + high * (genes // places) + turn
    return own[:, :1].astype(jnp.int32), rank, at, part, row


def cover_kernel(at_ref, spots_ref, starts_ref, lengths_ref, cover_ref, turned_ref):
    windows, exons, genes = starts_ref.shape
    rows, width = cover_ref.shape
    bins = width // windows
    position = lax.broadcasted_iota(jnp.int32, (bins, genes), 0) + at_ref[0] * bins
    lane = lax.broadcasted_iota(jnp.int32, (genes, rows), 1)
    for w in range(windows):
        spot = jnp.where(spots_ref[:, w : w + 1] == lane, 1.0, 0.0).astype(BF16)
        base = jnp.zeros((bins, genes), F32)
        for e in range(exons):
            past = position - starts_ref[w, e : e + 1, :]
            base += jnp.where((past >= 0) & (past < lengths_ref[w, e : e + 1, :]), 1.0, 0.0)
        turned = jnp.dot(base.astype(BF16), spot, preferred_element_type=F32)
        turned_ref[w * bins : (w + 1) * bins, :] = turned.astype(BF16)
        cover_ref[:, w * bins : (w + 1) * bins] = turned.T.astype(BF16)


def plan_kernel(places, at_ref, owner_ref, counts_ref, target_ref, keep_ref, pick_ref, mine_ref, spots_ref):
    windows, genes = owner_ref.shape
    capacity, tracks = counts_ref.shape[1:]
    side, sent_rows = target_ref.shape[:2]
    rows = mine_ref.shape[1]
    set_rows, sources = pick_ref.shape
    axis, column = at_ref[2], at_ref[5]
    lane = lax.broadcasted_iota(jnp.int32, (genes, rows), 1)
    targets = jnp.zeros((side * sent_rows, tracks), F32)
    keep = jnp.zeros(keep_ref.shape, F32)
    pick = jnp.zeros((set_rows, sources), F32)
    across = (((0,), (0,)), ((), ()))
    for w in range(windows):
        key, rank, at, part, row = ordering(at_ref, owner_ref, w, places, side, set_rows)
        spot = jnp.where(part * set_rows + row == lane, 1.0, 0.0)
        spots_ref[:, w : w + 1] = part * set_rows + row
        second = key // side
        first = key - second * side
        spare = w * capacity + (at // side) % capacity
        ours = part == axis
        here = jnp.where(ours & (row == lane[:, :set_rows]), 1.0, 0.0).astype(BF16)
        source = second * (sources // side) + spare
        origin = jnp.where(source == lane[:, :sources], 1.0, 0.0).astype(BF16)
        pick += lax.dot_general(here, origin, across, preferred_element_type=F32)
        room = lane[:, : keep_ref.shape[0]]
        here = jnp.where(ours & (second == column) & (spare == room), 1.0, 0.0).astype(BF16)
        origin = jnp.where(first * sent_rows + w == lane[:, : side * sent_rows], 1.0, 0.0).astype(BF16)
        keep += lax.dot_general(here, origin, across, preferred_element_type=F32)

        owned = (first == axis) & (second == column)
        coded = jnp.zeros((genes, tracks), F32)
        for k in range(capacity):
            slot = owned & (rank == k)
            filled = jnp.sum(jnp.where(slot, 1.0, 0.0), axis=0, keepdims=True) > 0
            count = counts_ref[w, k : k + 1, :]
            count = spread(jnp.where(jnp.broadcast_to(filled, count.shape), count, 1.0))
            coded += jnp.where(jnp.broadcast_to(slot, coded.shape), jnp.broadcast_to(count, coded.shape), 0.0)
            mark = jnp.where(jnp.broadcast_to(slot, lane.shape), spot, 0.0)
            mine_ref[w * capacity + k : w * capacity + k + 1, :] = jnp.sum(mark, axis=0, keepdims=True)
        goes = jnp.where(part * sent_rows + w == lane[:, : side * sent_rows], 1.0, 0.0).astype(BF16)
        targets += lax.dot_general(goes, coded.astype(BF16), across, preferred_element_type=F32)
    target_ref[...] = targets.reshape(side, sent_rows, tracks).astype(BF16)
    keep_ref[...] = keep.astype(BF16)
    pick_ref[...] = pick.astype(BF16)


def half_product(core, ref, head_ref):
    xs, windows, _, bins = ref.shape
    columns = [jnp.concatenate([ref[x, w] for w in range(windows)], axis=1) for x in range(xs)]
    weights = [head_ref[2 * x + core] for x in range(xs)]
    return lax.dot_general(
        jnp.concatenate(columns, axis=0),
        jnp.concatenate(weights, axis=0),
        (((0,), (0,)), ((), ())),
        preferred_element_type=F32,
    )


def half_kernel(at_ref, ours_ref, head_ref, logits_ref):
    logits_ref[...] = half_product(at_ref[1], ours_ref, head_ref)


def forward_kernel(
    at_ref, half_ref, other_ref, head_ref, cover_ref, target_ref, sent_ref, slope_ref, pred_ref
):
    side, sent_rows, tracks = sent_ref.shape
    set_rows = sent_rows - target_ref.shape[1]
    logits = half_ref[...] + half_product(1 - at_ref[1], other_ref, head_ref)
    low = jnp.exp(-jnp.abs(logits))
    above = 1.0 + low
    series = low * (1.0 - low * (0.5 - low * (1.0 / 3.0)))
    tail = jnp.where(low < 2.0**-7, series, jnp.log(above))
    pred_ref[...] = (jnp.maximum(logits, 0.0) + tail).astype(BF16)
    slope_ref[...] = jnp.where(logits >= 0, 1.0, low) / above
    partial = jnp.dot(cover_ref[...], pred_ref[...], preferred_element_type=F32)
    sent_ref[:, :set_rows, :] = packed_sum(partial).reshape(side, set_rows, tracks).astype(BF16)
    sent_ref[:, set_rows:, :] = target_ref[...]


def second_kernel(windows, got_ref, keep_ref, sent_ref):
    side, got_rows, tracks = got_ref.shape
    set_rows = got_rows - 2 * windows
    total = unpacked_sum(got_ref[0, :set_rows, :].astype(F32))
    for i in range(1, side):
        total += unpacked_sum(got_ref[i, :set_rows, :].astype(F32))
    rows = got_ref[:, set_rows:, :].astype(F32).reshape(keep_ref.shape[1], tracks).astype(BF16)
    kept = jnp.dot(keep_ref[...], rows, preferred_element_type=F32)
    block = jnp.concatenate([packed_sum(total), kept], axis=0).astype(BF16)
    for i in range(side):
        sent_ref[i] = block


def third_kernel(windows, got_ref, pick_ref, sent_ref):
    side, got_rows, tracks = got_ref.shape
    set_rows, sources = pick_ref.shape
    gene_pred = unpacked_sum(got_ref[0, :set_rows, :].astype(F32))
    for i in range(1, side):
        gene_pred += unpacked_sum(got_ref[i, :set_rows, :].astype(F32))
    rows = got_ref[:, set_rows:, :].astype(F32).reshape(sources, tracks).astype(BF16)
    gene_target = unspread(jnp.dot(pick_ref[...], rows, preferred_element_type=F32))
    total, target_sum, fit = [
        jnp.sum(values.reshape(windows, set_rows // windows, tracks), axis=1)
        for values in (gene_pred, gene_target, gene_target * jnp.log(gene_pred))
    ]
    target_sum = spread(target_sum, MIDDLE * (set_rows // windows))
    pieces = [squared(gene_target / gene_pred), *split(total), target_sum, fit]
    block = jnp.concatenate(pieces, axis=0).astype(BF16)
    for i in range(side):
        sent_ref[i] = block


def backward_kernel(
    genes, at_ref, got_ref, turned_ref, slope_ref, ours_ref, other_ref, mine_ref, counts_ref, sent_ref, loss_ref, gene_ref
):
    side, got_rows, tracks = got_ref.shape
    xs, windows, depth, bins = ours_ref.shape
    set_rows = got_rows - 4 * windows
    window_rows = set_rows // windows
    padded = sent_ref.shape[1]
    sums = got_ref[:, set_rows:, :].astype(F32)
    high, low, target_sum, fit = [sums[:, i * windows : (i + 1) * windows, :] for i in range(4)]
    total = jnp.sum(high, axis=0) + jnp.sum(low, axis=0)
    target_sum = jnp.sum(unspread(target_sum, MIDDLE * window_rows), axis=0)
    fit = jnp.sum(fit, axis=0)
    log_total = jnp.log(total)
    loss_ref[...] = (-fit + target_sum * log_total + 0.2 * (total - target_sum * log_total)) / target_sum
    scale = genes / target_sum
    level = scale * (0.2 + 0.8 * target_sum / total)
    grads = []
    for w in range(windows):
        ratio = rooted(got_ref[:, w * window_rows : (w + 1) * window_rows, :].astype(F32))
        grads.append(level[w : w + 1][None] - scale[w : w + 1][None] * ratio)
    gene_grad = jnp.concatenate(grads, axis=1).reshape(side * set_rows, tracks).astype(BF16)
    bin_grad = jnp.dot(turned_ref[...], gene_grad, preferred_element_type=F32)
    logit_grad = (bin_grad * slope_ref[...]).astype(BF16)

    capacity = counts_ref.shape[1]
    ratios = got_ref[:, :set_rows, :].reshape(side * set_rows, tracks)
    back = jnp.dot(mine_ref[...].astype(BF16), ratios, preferred_element_type=F32)
    filled = jnp.sum(mine_ref[...], axis=1, keepdims=True) > 0
    back = rooted(jnp.where(jnp.broadcast_to(filled, back.shape), back, 1.0))
    back = jnp.where(jnp.broadcast_to(filled, back.shape), 1.0 / back, 0.0)
    for w in range(windows):
        here = back[w * capacity : (w + 1) * capacity]
        gene_ref[w] = jnp.where(here > 0, counts_ref[w] * here, 0.0)

    core = at_ref[1]
    for ref, low in ((ours_ref, core), (other_ref, 1 - core)):
        lhs = [jnp.concatenate([ref[x, w] for w in range(windows)], axis=1) for x in range(xs)]
        grad = jnp.dot(jnp.concatenate(lhs, axis=0), logit_grad, preferred_element_type=F32).astype(BF16)
        for x in range(xs):
            for i in range(side):
                place = (2 * x + low) * at_ref[3] + i * at_ref[4]
                row = x * depth + i * padded
                sent_ref[place] = grad[row : row + padded]


def fold_kernel(got_ref, sent_ref):
    for i in range(sent_ref.shape[0]):
        total = got_ref[0, i].astype(F32)
        for j in range(1, got_ref.shape[0]):
            total += got_ref[j, i].astype(F32)
        sent_ref[i] = (total * jnp.abs(total)).astype(BF16)


def finish_kernel(got_ref, grad_ref):
    block = grad_ref.shape[0]
    total = jnp.zeros(got_ref.shape[1:], F32)
    for i in range(got_ref.shape[0]):
        grad = got_ref[i].astype(F32)
        root = jnp.sqrt(jnp.abs(grad))
        total += jnp.where(grad < 0, -root, root)
    grad_ref[...] = total[:block]


def per_device(embeddings, head, exon_starts, exon_lengths, gene_owner, gene_targets):
    places = lax.axis_size(SEQ)
    place = lax.axis_index(SEQ)
    core = lax.axis_index("c")
    side = lax.axis_size("y")
    windows, bin_dev, channels_dev = embeddings.shape
    channels, tracks = head.shape
    genes = gene_owner.shape[1]
    capacity = gene_targets.shape[1]
    held = genes // places
    per_place = windows * held
    rows = places * per_place
    xs, cores = lax.axis_size("x"), lax.axis_size("c")
    parts = xs * cores
    block = channels // places
    padded = -(-block // 16) * 16
    blocks_dev = channels_dev // block
    depth = blocks_dev * padded
    set_rows = rows // side
    side_rows = 2 * windows
    ahead, after = mixed_groups((side, places // side, xs, cores))

    packed = pl.pallas_call(
        lambda *refs: pack_kernel(block, padded, *refs),
        out_shape=jax.ShapeDtypeStruct((xs, windows, depth, bin_dev), BF16),
        in_specs=[HBM],
        out_specs=HBM,
        scratch_shapes=[
            pltpu.VMEM((windows, channels_dev, bin_dev), BF16),
            pltpu.VMEM((windows, depth, bin_dev), BF16),
            pltpu.SemaphoreType.DMA((windows,)),
            pltpu.SemaphoreType.DMA((windows, xs)),
        ],
        name="pack",
    )(embeddings.transpose(0, 2, 1))
    ours = exchange(packed, "x")

    padded_head = jnp.pad(head.reshape(places, block, tracks), ((0, 0), (0, padded - block), (0, 0)))
    padded_head = padded_head.reshape(parts, depth, tracks)

    first = core == 0
    y, z = lax.axis_index("y"), lax.axis_index("z")
    axis, column = jnp.where(first, y, z), jnp.where(first, z, y)
    at = jnp.stack([place, core, axis, jnp.where(first, side, 1), jnp.where(first, 1, side), column])
    at = at.astype(jnp.int32)

    plan = pl.pallas_call(
        lambda *refs: plan_kernel(places, *refs),
        out_shape=[
            jax.ShapeDtypeStruct((side, side_rows, tracks), BF16),
            jax.ShapeDtypeStruct((windows * capacity, side * side_rows), BF16),
            jax.ShapeDtypeStruct((set_rows, side * windows * capacity), BF16),
            jax.ShapeDtypeStruct((windows * capacity, rows), F32),
            jax.ShapeDtypeStruct((genes, 128), jnp.int32),
        ],
        in_specs=[SMEM, VMEM, VMEM],
        out_specs=[VMEM] * 5,
        compiler_params=SMALL,
        name="plan",
    )(at, gene_owner, gene_targets)
    ours, padded_head, plan, starts, lengths = lax.optimization_barrier(
        (ours, padded_head, tuple(plan), exon_starts.transpose(0, 2, 1), exon_lengths.transpose(0, 2, 1))
    )
    target_rows, keep, pick, mine, spots = plan
    other = lax.ppermute(ours, "c", [(0, 1), (1, 0)])
    cover, turned = pl.pallas_call(
        cover_kernel,
        out_shape=[
            jax.ShapeDtypeStruct((rows, windows * bin_dev), BF16),
            jax.ShapeDtypeStruct((windows * bin_dev, rows), BF16),
        ],
        in_specs=[SMEM] + [VMEM] * 3,
        out_specs=[VMEM] * 2,
        compiler_params=SMALL,
        name="cover",
    )(at, spots, starts, lengths)

    half = pl.pallas_call(
        half_kernel,
        out_shape=jax.ShapeDtypeStruct((windows * bin_dev, tracks), F32),
        in_specs=[SMEM, VMEM, VMEM],
        out_specs=VMEM,
        compiler_params=SMALL,
        name="half",
    )(at, ours, padded_head)

    sent, slope = pl.pallas_call(
        forward_kernel,
        out_shape=[
            jax.ShapeDtypeStruct((side, set_rows + side_rows, tracks), BF16),
            jax.ShapeDtypeStruct((windows * bin_dev, tracks), F32),
        ],
        in_specs=[SMEM] + [VMEM] * 5,
        out_specs=[VMEM] * 2,
        scratch_shapes=[pltpu.VMEM((windows * bin_dev, tracks), BF16)],
        compiler_params=SMALL,
        name="forward",
    )(at, half, other, padded_head, cover, target_rows)

    sent = pl.pallas_call(
        lambda *refs: second_kernel(windows, *refs),
        out_shape=jax.ShapeDtypeStruct((side, set_rows + windows * capacity, tracks), BF16),
        in_specs=[VMEM, VMEM],
        out_specs=VMEM,
        compiler_params=SMALL,
        name="second",
    )(exchange(sent, EVERY, ahead), keep)
    sent = pl.pallas_call(
        lambda *refs: third_kernel(windows, *refs),
        out_shape=jax.ShapeDtypeStruct((side, set_rows + 4 * windows, tracks), BF16),
        in_specs=[VMEM, VMEM],
        out_specs=VMEM,
        compiler_params=SMALL,
        name="third",
    )(exchange(sent, EVERY, after), pick)
    got = exchange(sent, EVERY, ahead)

    sent, loss, gene_here = pl.pallas_call(
        lambda *refs: backward_kernel(genes, *refs),
        out_shape=[
            jax.ShapeDtypeStruct((places, padded, tracks), BF16),
            jax.ShapeDtypeStruct((windows, tracks), F32),
            jax.ShapeDtypeStruct(gene_targets.shape, F32),
        ],
        in_specs=[SMEM] + [VMEM] * 7,
        out_specs=[VMEM] * 3,
        compiler_params=SMALL,
        name="backward",
    )(at, got, turned, slope, ours, other, mine, gene_targets)

    summed = exchange(sent.reshape(side, side * padded, tracks), EVERY, ahead)
    summed = pl.pallas_call(
        fold_kernel,
        out_shape=jax.ShapeDtypeStruct((side, padded, tracks), BF16),
        in_specs=[VMEM],
        out_specs=VMEM,
        compiler_params=SMALL,
        name="fold",
    )(summed.reshape(side, side, padded, tracks))
    grad_head = pl.pallas_call(
        finish_kernel,
        out_shape=jax.ShapeDtypeStruct((block, tracks), F32),
        in_specs=[VMEM],
        out_specs=VMEM,
        compiler_params=SMALL,
        name="finish",
    )(exchange(summed, EVERY, after))
    return (gene_here, loss, grad_head)


def solution(mesh):
    shape = (8, 8, 4, 2)
    fine = Mesh(mesh.devices.reshape(shape), EVERY)
    return jax.shard_map(
        per_device,
        mesh=fine,
        in_specs=(P(None, SEQ, ("x", "c")), P(None, ("x", "c")), P(), P(), P(), P(None, SEQ, ("x", "c"))),
        out_specs=(P(None, SEQ, ("x", "c")), P(None, ("x", "c")), P(SEQ, ("x", "c"))),
        check_vma=False,
    )
```

```python
import jax
import jax.numpy as jnp
import numpy as np
from jax import lax
from jax.experimental import pallas as pl
from jax.experimental.pallas import tpu as pltpu
from jax.sharding import Mesh, PartitionSpec as P

SEQ = ("y", "z")
EVERY = ("y", "z", "x", "c")
F32 = jnp.float32
BF16 = jnp.bfloat16
MIDDLE = 28.28
VMEM = pl.BlockSpec(memory_space=pltpu.VMEM)
SMEM = pl.BlockSpec(memory_space=pltpu.SMEM)
HBM = pl.BlockSpec(memory_space=pltpu.HBM)
SMALL = pltpu.CompilerParams(vmem_limit_bytes=16 * 1024 * 1024)


def exchange(blocks, axes, groups=None):
    return lax.all_to_all(blocks, axes, split_axis=0, concat_axis=0, axis_index_groups=groups, tiled=True)


def mixed_groups(shape):
    ids = np.arange(int(np.prod(shape))).reshape(shape)
    ahead, after = [], []
    for x in range(shape[2]):
        for k in range(shape[0]):
            ahead += [ids[:, k, x, 0].tolist(), ids[k, :, x, 1].tolist()]
            after += [ids[k, :, x, 0].tolist(), ids[:, k, x, 1].tolist()]
    return ahead, after


def root_of(values):
    return values * lax.rsqrt(jnp.maximum(values, 2.0**-126))


def spread(counts, middle=MIDDLE):
    scaled = counts * (1.0 / middle)
    for _ in range(4):
        scaled = scaled * scaled
    return scaled


def unspread(coded, middle=MIDDLE):
    for _ in range(4):
        coded = jnp.sqrt(coded)
    return coded * middle


def squared(ratio):
    small = ratio < 2.0**63
    scaled = jnp.where(small, ratio, ratio * 2.0**-96)
    return jnp.where(small, scaled * scaled, -(scaled * scaled))


def rooted(coded):
    root = root_of(jnp.abs(coded))
    return jnp.where(coded < 0, root * 2.0**96, root)


def split(values):
    high = values.astype(BF16).astype(F32)
    return high, values - high


def packed_sum(partial):
    tiny = partial < 2.0**-40
    scaled = jnp.where(tiny, partial * 2.0**80, partial)
    return jnp.where(tiny, -(scaled * scaled), scaled * scaled)


def unpacked_sum(coded):
    root = root_of(jnp.abs(coded))
    return jnp.where(coded < 0, root * 2.0**-80, root)


def pack_kernel(block, padded, local_ref, packed_ref, raw_ref, rows_ref, arrived, left):
    copies, windows, depth, bins = packed_ref.shape
    reads = [pltpu.make_async_copy(local_ref.at[w], raw_ref.at[w], arrived.at[w]) for w in range(windows)]
    for read in reads:
        read.start()
    writes = []
    for w in range(windows):
        reads[w].wait()
        rows = raw_ref[w].astype(F32)
        gap = jnp.zeros((padded - block, bins), F32)
        pieces = []
        for i in range(depth // padded):
            pieces += [rows[i * block : (i + 1) * block], gap]
        rows_ref[w] = jnp.concatenate(pieces, axis=0).astype(BF16)
        for i in range(copies):
            write = pltpu.make_async_copy(rows_ref.at[w], packed_ref.at[i, w], left.at[w, i])
            write.start()
            writes.append(write)
    for write in writes:
        write.wait()


def ordering(at_ref, owner_ref, w, places, side, set_rows):
    windows, genes = owner_ref.shape
    square = (genes, genes)
    owner = owner_ref[w : w + 1, :]
    high = owner // side
    key = jnp.where(at_ref[1] == 0, (owner - high * side) * side + high, owner)
    other = jnp.broadcast_to(key.astype(F32), square)
    own = other.T
    earlier = lax.broadcasted_iota(jnp.int32, square, 1) < lax.broadcasted_iota(jnp.int32, square, 0)
    ahead = jnp.where((other == own) & earlier, 1.0, 0.0)
    rank = jnp.sum(ahead, axis=1, keepdims=True)
    at = jnp.sum(jnp.where(other < own, 1.0, ahead), axis=1, keepdims=True).astype(jnp.int32)
    turn = at // places
    place_of = at - turn * places
    high = place_of // side
    part = place_of - high * side
    row = w * (set_rows // windows) + high * (genes // places) + turn
    return own[:, :1].astype(jnp.int32), rank, at, part, row


def cover_kernel(at_ref, spots_ref, starts_ref, lengths_ref, cover_ref, turned_ref):
    windows, exons, genes = starts_ref.shape
    rows, width = cover_ref.shape
    bins = width // windows
    position = lax.broadcasted_iota(jnp.int32, (bins, genes), 0) + at_ref[0] * bins
    lane = lax.broadcasted_iota(jnp.int32, (genes, rows), 1)
    for w in range(windows):
        spot = jnp.where(spots_ref[:, w : w + 1] == lane, 1.0, 0.0).astype(BF16)
        base = jnp.zeros((bins, genes), F32)
        for e in range(exons):
            past = position - starts_ref[w, e : e + 1, :]
            base += jnp.where((past >= 0) & (past < lengths_ref[w, e : e + 1, :]), 1.0, 0.0)
        turned = jnp.dot(base.astype(BF16), spot, preferred_element_type=F32)
        turned_ref[w * bins : (w + 1) * bins, :] = turned.astype(BF16)
        cover_ref[:, w * bins : (w + 1) * bins] = turned.T.astype(BF16)


def plan_kernel(places, at_ref, owner_ref, counts_ref, target_ref, keep_ref, pick_ref, mine_ref, spots_ref):
    windows, genes = owner_ref.shape
    capacity, tracks = counts_ref.shape[1:]
    side, sent_rows = target_ref.shape[:2]
    rows = mine_ref.shape[1]
    set_rows, sources = pick_ref.shape
    axis, column = at_ref[2], at_ref[5]
    lane = lax.broadcasted_iota(jnp.int32, (genes, rows), 1)
    targets = jnp.zeros((side * sent_rows, tracks), F32)
    keep = jnp.zeros(keep_ref.shape, F32)
    pick = jnp.zeros((set_rows, sources), F32)
    across = (((0,), (0,)), ((), ()))
    for w in range(windows):
        key, rank, at, part, row = ordering(at_ref, owner_ref, w, places, side, set_rows)
        spot = jnp.where(part * set_rows + row == lane, 1.0, 0.0)
        spots_ref[:, w : w + 1] = part * set_rows + row
        second = key // side
        first = key - second * side
        spare = w * capacity + (at // side) % capacity
        ours = part == axis
        here = jnp.where(ours & (row == lane[:, :set_rows]), 1.0, 0.0).astype(BF16)
        source = second * (sources // side) + spare
        origin = jnp.where(source == lane[:, :sources], 1.0, 0.0).astype(BF16)
        pick += lax.dot_general(here, origin, across, preferred_element_type=F32)
        room = lane[:, : keep_ref.shape[0]]
        here = jnp.where(ours & (second == column) & (spare == room), 1.0, 0.0).astype(BF16)
        origin = jnp.where(first * sent_rows + w == lane[:, : side * sent_rows], 1.0, 0.0).astype(BF16)
        keep += lax.dot_general(here, origin, across, preferred_element_type=F32)

        owned = (first == axis) & (second == column)
        coded = jnp.zeros((genes, tracks), F32)
        for k in range(capacity):
            slot = owned & (rank == k)
            filled = jnp.sum(jnp.where(slot, 1.0, 0.0), axis=0, keepdims=True) > 0
            count = counts_ref[w, k : k + 1, :]
            count = spread(jnp.where(jnp.broadcast_to(filled, count.shape), count, 1.0))
            coded += jnp.where(jnp.broadcast_to(slot, coded.shape), jnp.broadcast_to(count, coded.shape), 0.0)
            mark = jnp.where(jnp.broadcast_to(slot, lane.shape), spot, 0.0)
            mine_ref[w * capacity + k : w * capacity + k + 1, :] = jnp.sum(mark, axis=0, keepdims=True)
        goes = jnp.where(part * sent_rows + w == lane[:, : side * sent_rows], 1.0, 0.0).astype(BF16)
        targets += lax.dot_general(goes, coded.astype(BF16), across, preferred_element_type=F32)
    target_ref[...] = targets.reshape(side, sent_rows, tracks).astype(BF16)
    keep_ref[...] = keep.astype(BF16)
    pick_ref[...] = pick.astype(BF16)


def half_product(core, ref, head_ref):
    xs, windows, _, bins = ref.shape
    columns = [jnp.concatenate([ref[x, w] for w in range(windows)], axis=1) for x in range(xs)]
    weights = [head_ref[2 * x + core] for x in range(xs)]
    return lax.dot_general(
        jnp.concatenate(columns, axis=0),
        jnp.concatenate(weights, axis=0),
        (((0,), (0,)), ((), ())),
        preferred_element_type=F32,
    )


def half_kernel(at_ref, ours_ref, head_ref, logits_ref):
    logits_ref[...] = half_product(at_ref[1], ours_ref, head_ref)


def forward_kernel(
    at_ref, half_ref, other_ref, head_ref, cover_ref, target_ref, sent_ref, slope_ref, pred_ref
):
    side, sent_rows, tracks = sent_ref.shape
    set_rows = sent_rows - target_ref.shape[1]
    logits = half_ref[...] + half_product(1 - at_ref[1], other_ref, head_ref)
    low = jnp.exp(-jnp.abs(logits))
    above = 1.0 + low
    series = low * (1.0 - low * (0.5 - low * (1.0 / 3.0)))
    tail = jnp.where(low < 2.0**-7, series, jnp.log(above))
    pred_ref[...] = (jnp.maximum(logits, 0.0) + tail).astype(BF16)
    slope_ref[...] = jnp.where(logits >= 0, 1.0, low) / above
    partial = jnp.dot(cover_ref[...], pred_ref[...], preferred_element_type=F32)
    sent_ref[:, :set_rows, :] = packed_sum(partial).reshape(side, set_rows, tracks).astype(BF16)
    sent_ref[:, set_rows:, :] = target_ref[...]


def second_kernel(windows, got_ref, keep_ref, sent_ref):
    side, got_rows, tracks = got_ref.shape
    set_rows = got_rows - 2 * windows
    total = unpacked_sum(got_ref[0, :set_rows, :].astype(F32))
    for i in range(1, side):
        total += unpacked_sum(got_ref[i, :set_rows, :].astype(F32))
    rows = got_ref[:, set_rows:, :].astype(F32).reshape(keep_ref.shape[1], tracks).astype(BF16)
    kept = jnp.dot(keep_ref[...], rows, preferred_element_type=F32)
    block = jnp.concatenate([packed_sum(total), kept], axis=0).astype(BF16)
    for i in range(side):
        sent_ref[i] = block


def third_kernel(windows, got_ref, pick_ref, sent_ref):
    side, got_rows, tracks = got_ref.shape
    set_rows, sources = pick_ref.shape
    gene_pred = unpacked_sum(got_ref[0, :set_rows, :].astype(F32))
    for i in range(1, side):
        gene_pred += unpacked_sum(got_ref[i, :set_rows, :].astype(F32))
    rows = got_ref[:, set_rows:, :].astype(F32).reshape(sources, tracks).astype(BF16)
    gene_target = unspread(jnp.dot(pick_ref[...], rows, preferred_element_type=F32))
    total, target_sum, fit = [
        jnp.sum(values.reshape(windows, set_rows // windows, tracks), axis=1)
        for values in (gene_pred, gene_target, gene_target * jnp.log(gene_pred))
    ]
    target_sum = spread(target_sum, MIDDLE * (set_rows // windows))
    pieces = [squared(gene_target / gene_pred), *split(total), target_sum, fit]
    block = jnp.concatenate(pieces, axis=0).astype(BF16)
    for i in range(side):
        sent_ref[i] = block


def backward_kernel(
    genes, at_ref, got_ref, turned_ref, slope_ref, ours_ref, other_ref, mine_ref, counts_ref, sent_ref, loss_ref, gene_ref
):
    side, got_rows, tracks = got_ref.shape
    xs, windows, depth, bins = ours_ref.shape
    set_rows = got_rows - 4 * windows
    window_rows = set_rows // windows
    padded = sent_ref.shape[1]
    sums = got_ref[:, set_rows:, :].astype(F32)
    high, low, target_sum, fit = [sums[:, i * windows : (i + 1) * windows, :] for i in range(4)]
    total = jnp.sum(high, axis=0) + jnp.sum(low, axis=0)
    target_sum = jnp.sum(unspread(target_sum, MIDDLE * window_rows), axis=0)
    fit = jnp.sum(fit, axis=0)
    log_total = jnp.log(total)
    loss_ref[...] = (-fit + target_sum * log_total + 0.2 * (total - target_sum * log_total)) / target_sum
    scale = genes / target_sum
    level = scale * (0.2 + 0.8 * target_sum / total)
    grads = []
    for w in range(windows):
        ratio = rooted(got_ref[:, w * window_rows : (w + 1) * window_rows, :].astype(F32))
        grads.append(level[w : w + 1][None] - scale[w : w + 1][None] * ratio)
    gene_grad = jnp.concatenate(grads, axis=1).reshape(side * set_rows, tracks).astype(BF16)
    bin_grad = jnp.dot(turned_ref[...], gene_grad, preferred_element_type=F32)
    logit_grad = (bin_grad * slope_ref[...]).astype(BF16)

    capacity = counts_ref.shape[1]
    ratios = got_ref[:, :set_rows, :].reshape(side * set_rows, tracks)
    back = jnp.dot(mine_ref[...].astype(BF16), ratios, preferred_element_type=F32)
    filled = jnp.sum(mine_ref[...], axis=1, keepdims=True) > 0
    back = rooted(jnp.where(jnp.broadcast_to(filled, back.shape), back, 1.0))
    back = jnp.where(jnp.broadcast_to(filled, back.shape), 1.0 / back, 0.0)
    for w in range(windows):
        here = back[w * capacity : (w + 1) * capacity]
        gene_ref[w] = jnp.where(here > 0, counts_ref[w] * here, 0.0)

    core = at_ref[1]
    for ref, low in ((ours_ref, core), (other_ref, 1 - core)):
        lhs = [jnp.concatenate([ref[x, w] for w in range(windows)], axis=1) for x in range(xs)]
        grad = jnp.dot(jnp.concatenate(lhs, axis=0), logit_grad, preferred_element_type=F32).astype(BF16)
        for x in range(xs):
            for i in range(side):
                place = (2 * x + low) * at_ref[3] + i * at_ref[4]
                row = x * depth + i * padded
                sent_ref[place] = grad[row : row + padded]


def fold_kernel(got_ref, sent_ref):
    for i in range(sent_ref.shape[0]):
        total = got_ref[0, i].astype(F32)
        for j in range(1, got_ref.shape[0]):
            total += got_ref[j, i].astype(F32)
        sent_ref[i] = (total * jnp.abs(total)).astype(BF16)


def finish_kernel(got_ref, grad_ref):
    block = grad_ref.shape[0]
    total = jnp.zeros(got_ref.shape[1:], F32)
    for i in range(got_ref.shape[0]):
        grad = got_ref[i].astype(F32)
        root = root_of(jnp.abs(grad))
        total += jnp.where(grad < 0, -root, root)
    grad_ref[...] = total[:block]


def per_device(embeddings, head, exon_starts, exon_lengths, gene_owner, gene_targets):
    places = lax.axis_size(SEQ)
    place = lax.axis_index(SEQ)
    core = lax.axis_index("c")
    side = lax.axis_size("y")
    windows, bin_dev, channels_dev = embeddings.shape
    channels, tracks = head.shape
    genes = gene_owner.shape[1]
    capacity = gene_targets.shape[1]
    held = genes // places
    per_place = windows * held
    rows = places * per_place
    xs, cores = lax.axis_size("x"), lax.axis_size("c")
    parts = xs * cores
    block = channels // places
    padded = -(-block // 16) * 16
    blocks_dev = channels_dev // block
    depth = blocks_dev * padded
    set_rows = rows // side
    side_rows = 2 * windows
    ahead, after = mixed_groups((side, places // side, xs, cores))

    packed = pl.pallas_call(
        lambda *refs: pack_kernel(block, padded, *refs),
        out_shape=jax.ShapeDtypeStruct((xs, windows, depth, bin_dev), BF16),
        in_specs=[HBM],
        out_specs=HBM,
        scratch_shapes=[
            pltpu.VMEM((windows, channels_dev, bin_dev), BF16),
            pltpu.VMEM((windows, depth, bin_dev), BF16),
            pltpu.SemaphoreType.DMA((windows,)),
            pltpu.SemaphoreType.DMA((windows, xs)),
        ],
        name="pack",
    )(embeddings.transpose(0, 2, 1))
    ours = exchange(packed, "x")

    padded_head = jnp.pad(head.reshape(places, block, tracks), ((0, 0), (0, padded - block), (0, 0)))
    padded_head = padded_head.reshape(parts, depth, tracks)

    first = core == 0
    y, z = lax.axis_index("y"), lax.axis_index("z")
    axis, column = jnp.where(first, y, z), jnp.where(first, z, y)
    at = jnp.stack([place, core, axis, jnp.where(first, side, 1), jnp.where(first, 1, side), column])
    at = at.astype(jnp.int32)

    plan = pl.pallas_call(
        lambda *refs: plan_kernel(places, *refs),
        out_shape=[
            jax.ShapeDtypeStruct((side, side_rows, tracks), BF16),
            jax.ShapeDtypeStruct((windows * capacity, side * side_rows), BF16),
            jax.ShapeDtypeStruct((set_rows, side * windows * capacity), BF16),
            jax.ShapeDtypeStruct((windows * capacity, rows), F32),
            jax.ShapeDtypeStruct((genes, 128), jnp.int32),
        ],
        in_specs=[SMEM, VMEM, VMEM],
        out_specs=[VMEM] * 5,
        compiler_params=SMALL,
        name="plan",
    )(at, gene_owner, gene_targets)
    ours, padded_head, plan, starts, lengths = lax.optimization_barrier(
        (ours, padded_head, tuple(plan), exon_starts.transpose(0, 2, 1), exon_lengths.transpose(0, 2, 1))
    )
    target_rows, keep, pick, mine, spots = plan
    other = lax.ppermute(ours, "c", [(0, 1), (1, 0)])
    cover, turned = pl.pallas_call(
        cover_kernel,
        out_shape=[
            jax.ShapeDtypeStruct((rows, windows * bin_dev), BF16),
            jax.ShapeDtypeStruct((windows * bin_dev, rows), BF16),
        ],
        in_specs=[SMEM] + [VMEM] * 3,
        out_specs=[VMEM] * 2,
        compiler_params=SMALL,
        name="cover",
    )(at, spots, starts, lengths)

    half = pl.pallas_call(
        half_kernel,
        out_shape=jax.ShapeDtypeStruct((windows * bin_dev, tracks), F32),
        in_specs=[SMEM, VMEM, VMEM],
        out_specs=VMEM,
        compiler_params=SMALL,
        name="half",
    )(at, ours, padded_head)

    sent, slope = pl.pallas_call(
        forward_kernel,
        out_shape=[
            jax.ShapeDtypeStruct((side, set_rows + side_rows, tracks), BF16),
            jax.ShapeDtypeStruct((windows * bin_dev, tracks), F32),
        ],
        in_specs=[SMEM] + [VMEM] * 5,
        out_specs=[VMEM] * 2,
        scratch_shapes=[pltpu.VMEM((windows * bin_dev, tracks), BF16)],
        compiler_params=SMALL,
        name="forward",
    )(at, half, other, padded_head, cover, target_rows)

    sent = pl.pallas_call(
        lambda *refs: second_kernel(windows, *refs),
        out_shape=jax.ShapeDtypeStruct((side, set_rows + windows * capacity, tracks), BF16),
        in_specs=[VMEM, VMEM],
        out_specs=VMEM,
        compiler_params=SMALL,
        name="second",
    )(exchange(sent, EVERY, ahead), keep)
    sent = pl.pallas_call(
        lambda *refs: third_kernel(windows, *refs),
        out_shape=jax.ShapeDtypeStruct((side, set_rows + 4 * windows, tracks), BF16),
        in_specs=[VMEM, VMEM],
        out_specs=VMEM,
        compiler_params=SMALL,
        name="third",
    )(exchange(sent, EVERY, after), pick)
    got = exchange(sent, EVERY, ahead)

    sent, loss, gene_here = pl.pallas_call(
        lambda *refs: backward_kernel(genes, *refs),
        out_shape=[
            jax.ShapeDtypeStruct((places, padded, tracks), BF16),
            jax.ShapeDtypeStruct((windows, tracks), F32),
            jax.ShapeDtypeStruct(gene_targets.shape, F32),
        ],
        in_specs=[SMEM] + [VMEM] * 7,
        out_specs=[VMEM] * 3,
        compiler_params=SMALL,
        name="backward",
    )(at, got, turned, slope, ours, other, mine, gene_targets)

    summed = exchange(sent.reshape(side, side * padded, tracks), EVERY, ahead)
    summed = pl.pallas_call(
        fold_kernel,
        out_shape=jax.ShapeDtypeStruct((side, padded, tracks), BF16),
        in_specs=[VMEM],
        out_specs=VMEM,
        compiler_params=SMALL,
        name="fold",
    )(summed.reshape(side, side, padded, tracks))
    grad_head = pl.pallas_call(
        finish_kernel,
        out_shape=jax.ShapeDtypeStruct((block, tracks), F32),
        in_specs=[VMEM],
        out_specs=VMEM,
        compiler_params=SMALL,
        name="finish",
    )(exchange(summed, EVERY, after))
    return (gene_here, loss, grad_head)


def solution(mesh):
    shape = (8, 8, 4, 2)
    fine = Mesh(mesh.devices.reshape(shape), EVERY)
    return jax.shard_map(
        per_device,
        mesh=fine,
        in_specs=(P(None, SEQ, ("x", "c")), P(None, ("x", "c")), P(), P(), P(), P(None, SEQ, ("x", "c"))),
        out_specs=(P(None, SEQ, ("x", "c")), P(None, ("x", "c")), P(SEQ, ("x", "c"))),
        check_vma=False,
    )
```
